128 devices in a mesh: seq: 32 (over z, y, core), head: 4 (over x).
Axes of the slice: x: 4, y: 4, z: 4, core: 2. Of those that a mesh axis runs over, the one named last changes fastest.
Arguments:
- tokens: bfloat16 [16384, 4096], P('seq'), may hold values from -6 to 6
- w_query: bfloat16 [4096, 2048], P('seq', 'head'), may hold values from -0.09375 to 0.09375
- w_key: bfloat16 [4096, 2048], P('seq', 'head'), may hold values from -0.09375 to 0.09375
- w_value: bfloat16 [4096, 2048], P('seq', 'head'), may hold values from -0.09375 to 0.09375
- omega_seed: int32 [16, 128, 256], P('head'), may hold values from -4 to 4
- grad_out: bfloat16 [16384, 2048], P('seq', 'head'), may hold values from -6 to 6
Outputs:
- input_grad: bfloat16 [16384, 4096], P('seq', 'head')
- query_wgrad: float32 [4096, 2048], P('seq', 'head')
- key_wgrad: float32 [4096, 2048], P('seq', 'head')
- value_wgrad: float32 [4096, 2048], P('seq', 'head')
The draws below stay inside these ranges and needn't reach their ends.
Inputs may be any that keep to these rules, and one draw needn't show every extreme that they name: `omega_seed`: the feature seeds are small whole numbers.
All inputs are finite; a program needn't handle non-finite values.
Results may differ from the reference program's by a relative error of at most 0.02.
Values may be sent and summed in bfloat16 or wider, within the bound.
No kernel may reach another device: no remote copies, remote signals or barrier semaphores. Data moves between devices by JAX's collectives and lax.ppermute only.
A program may use at most 128 MiB of HBM per device.

```python
import math
import jax
import jax.numpy as jnp
from jax import lax

D = 4096
HD = 128
M = 256
TOK_DEV = 512
HEADS = 16
TOKENS = 16384
N_SEQ = 32


def plant(drawn, rng, smallest, top_value):
    longest = drawn.shape.index(max(drawn.shape))
    spots = []
    for shift in (0, 1):
        where = [jax.random.randint(jax.random.fold_in(rng, axis), (), 0, length) for axis, length in enumerate(drawn.shape)]
        where[longest] = (where[longest] + shift) % drawn.shape[longest]
        spots.append(tuple(where))
    return drawn.at[spots[0]].set(smallest).at[spots[1]].set(top_value)


def steps_of(own_key, dims, shards, low, top_value):
    def one(position, parts):
        steps = jax.random.uniform(jax.random.fold_in(jax.random.fold_in(own_key, 6), position), (parts,), jnp.float32, low / len(shards), top_value / len(shards))
        return jnp.repeat(jnp.exp(steps), dims[position] // parts).reshape((-1,) + (1,) * (len(dims) - position - 1))

    gain = one(*shards[0])
    for cut in shards[1:]:
        gain = gain * one(*cut)
    return gain


def gaussian(rng, dims, scale, limit, shards=(), dtype=jnp.bfloat16):
    array = scale * jax.random.normal(rng, dims, jnp.float32)
    if shards:
        array = array * steps_of(rng, dims, shards, -0.22, 0.18)
    return jnp.clip(array, -limit, limit).astype(dtype)


def setup_inputs(seed: int = 0) -> dict:
    keys = jax.random.split(jax.random.key(seed), 7)
    tokens = gaussian(keys[0], (TOKENS, D), 1.0, 6.0, ((0, 32),))
    w_query = gaussian(keys[1], (D, HEADS * HD), D ** -0.5, 0.09375, ((0, 32), (1, 4)))
    w_key = gaussian(keys[2], (D, HEADS * HD), D ** -0.5, 0.09375, ((0, 32), (1, 4)))
    w_value = gaussian(keys[3], (D, HEADS * HD), D ** -0.5, 0.09375, ((0, 32), (1, 4)))
    omega_seed = plant(jax.random.randint(keys[4], (HEADS, HD, M), -4, 5), jax.random.fold_in(keys[4], 1), -4, 4).astype(jnp.int32)
    grad_out = gaussian(keys[5], (TOKENS, HEADS * HD), 1.0, 6.0, ((0, 32), (1, 4)))
    return {"tokens": tokens, "w_query": w_query, "w_key": w_key, "w_value": w_value, "omega_seed": omega_seed, "grad_out": grad_out}


exact_arithmetic_mode = lax.Precision.HIGHEST
seed_step = 0.4

def feature_map(scaled, projection):
    projected = jnp.einsum('htd,hdm->htm', scaled, projection, precision=exact_arithmetic_mode)
    return jnp.exp(projected - 0.5 * lax.optimization_barrier(jnp.sum(scaled * scaled, -1, keepdims=True))) / math.sqrt(projection.shape[-1])

def feature_grad(upstream, features, scaled, projection):
    weighted = upstream * features
    projected = jnp.einsum('htm,hdm->htd', weighted, projection, precision=exact_arithmetic_mode)
    return (projected - lax.optimization_barrier(jnp.sum(weighted, -1, keepdims=True)) * scaled) * scaled.shape[-1] ** (-0.25)

def blocked(value_matrix):
    return value_matrix.astype(jnp.float32).reshape(N_SEQ, TOK_DEV, HEADS, HD).transpose(0, 2, 1, 3)

def unblocked(value_matrix):
    return value_matrix.transpose(0, 2, 1, 3).reshape(TOKENS, HEADS * HD).astype(jnp.bfloat16)

def back_product(grads, weight):
    return lax.dot_general(grads, weight, (((1,), (1,)), ((), ())), preferred_element_type=jnp.float32)

def reference(tokens, w_query, w_key, w_value, omega_seed, grad_out):
    query_act = jnp.dot(tokens, w_query, preferred_element_type=jnp.float32).astype(jnp.bfloat16)
    key_act = jnp.dot(tokens, w_key, preferred_element_type=jnp.float32).astype(jnp.bfloat16)
    value_act = jnp.dot(tokens, w_value, preferred_element_type=jnp.float32).astype(jnp.bfloat16)
    projection = omega_seed.astype(jnp.float32) * seed_step
    scale_in = HD ** (-0.25)
    query_scaled = blocked(query_act) * scale_in
    key_scaled = blocked(key_act) * scale_in
    value_matrix = blocked(value_act)
    upstream = blocked(grad_out)
    causal = jnp.tril(jnp.ones((TOK_DEV, TOK_DEV), jnp.float32))

    def forward_block(carry, inputs):
        prefix_carried_outer, prefix_normaliser_accrual = carry
        q_scaled, k_scaled, value_block_rows, grad_rows = inputs
        query_feature_rows = feature_map(q_scaled, projection)
        source_embedding_entries = feature_map(k_scaled, projection)
        attention_scores = jnp.einsum('htm,hsm->hts', query_feature_rows, source_embedding_entries, precision=exact_arithmetic_mode) * causal
        attention_numerator = jnp.einsum('xyw,xwc->xyc', attention_scores, value_block_rows, precision=exact_arithmetic_mode) + jnp.einsum('sji,six->sjx', query_feature_rows, prefix_carried_outer, precision=exact_arithmetic_mode)
        normer = lax.optimization_barrier(jnp.sum(attention_scores, -1)) + jnp.einsum('htm,hm->ht', query_feature_rows, prefix_normaliser_accrual, precision=exact_arithmetic_mode)
        output = attention_numerator / normer[..., None]
        dividend_cotangent = grad_rows / normer[..., None]
        normaliser_cotangent = -lax.optimization_barrier(jnp.sum(grad_rows * output, -1)) / normer
        couplewise_products = (jnp.einsum('htd,hsd->hts', dividend_cotangent, value_block_rows, precision=exact_arithmetic_mode) + normaliser_cotangent[..., None]) * causal
        target_embedding_cotangent = jnp.einsum('mez,mzo->meo', couplewise_products, source_embedding_entries, precision=exact_arithmetic_mode) + jnp.einsum('zrc,zfc->zrf', dividend_cotangent, prefix_carried_outer, precision=exact_arithmetic_mode) + normaliser_cotangent[..., None] * prefix_normaliser_accrual[:, None, :]
        query_grad = feature_grad(target_embedding_cotangent, query_feature_rows, q_scaled, projection)
        updated_states = prefix_carried_outer + jnp.einsum('vzn,vza->vna', source_embedding_entries, value_block_rows, precision=exact_arithmetic_mode)
        new_totals = prefix_normaliser_accrual + lax.optimization_barrier(jnp.sum(source_embedding_entries, 1))
        return ((updated_states, new_totals), (query_grad, dividend_cotangent, normaliser_cotangent))
    start_states = jnp.zeros((HEADS, M, HD), jnp.float32)
    start_totals = jnp.zeros((HEADS, M), jnp.float32)
    carried, results = lax.scan(forward_block, (start_states, start_totals), (query_scaled, key_scaled, value_matrix, upstream))
    query_grad, dividend_cotangent, normaliser_cotangent = results

    def backward_block(carry, inputs):
        subsequent_states, subsequent_sum = carry
        q_scaled, k_scaled, value_block_rows, numerator_rows, den_rows = inputs
        query_feature_rows = feature_map(q_scaled, projection)
        source_embedding_entries = feature_map(k_scaled, projection)
        attention_scores = jnp.einsum('htm,hsm->hts', query_feature_rows, source_embedding_entries, precision=exact_arithmetic_mode) * causal
        couplewise_products = (jnp.einsum('htd,hsd->hts', numerator_rows, value_block_rows, precision=exact_arithmetic_mode) + den_rows[..., None]) * causal
        key_feature_gradient = jnp.einsum('ykl,yku->ylu', couplewise_products, query_feature_rows, precision=exact_arithmetic_mode) + jnp.einsum('bgq,bxq->bgx', value_block_rows, subsequent_states, precision=exact_arithmetic_mode) + subsequent_sum[:, None, :]
        value_gradient_rows = jnp.einsum('vkm,vky->vmy', attention_scores, numerator_rows, precision=exact_arithmetic_mode) + jnp.einsum('tjr,tro->tjo', source_embedding_entries, subsequent_states, precision=exact_arithmetic_mode)
        key_grad = feature_grad(key_feature_gradient, source_embedding_entries, k_scaled, projection)
        updated_states = subsequent_states + jnp.einsum('opu,opc->ouc', query_feature_rows, numerator_rows, precision=exact_arithmetic_mode)
        new_sum = subsequent_sum + jnp.einsum('htm,ht->hm', query_feature_rows, den_rows, precision=exact_arithmetic_mode)
        return ((updated_states, new_sum), (key_grad, value_gradient_rows))
    carried_back, results_back = lax.scan(backward_block, (start_states, start_totals), (query_scaled, key_scaled, value_matrix, dividend_cotangent, normaliser_cotangent), reverse=True)
    key_grad, value_gradient_rows = results_back
    query16 = unblocked(query_grad)
    key16 = unblocked(key_grad)
    value16 = unblocked(value_gradient_rows)
    input_grad = (back_product(query16, w_query) + back_product(key16, w_key) + back_product(value16, w_value)).astype(jnp.bfloat16)
    joined = jnp.concatenate([query16, key16, value16], 1)
    token_blocks = tokens.reshape(N_SEQ, TOK_DEV, D)
    grad_blocks = joined.reshape(N_SEQ, TOK_DEV, 3 * HEADS * HD)

    def weight_block(total, pieces):
        token_rows, grad_rows = pieces
        partial_value = lax.dot_general(token_rows, grad_rows, (((0,), (0,)), ((), ())), preferred_element_type=jnp.float32)
        partial_value = lax.optimization_barrier(partial_value.astype(jnp.bfloat16)).astype(jnp.float32)
        return (total + partial_value, None)
    start_total = jnp.zeros((D, 3 * HEADS * HD), jnp.float32)
    weight_total, unused = lax.scan(weight_block, start_total, (token_blocks, grad_blocks))
    columns = HEADS * HD
    return (input_grad, weight_total[:, :columns], weight_total[:, columns:2 * columns], weight_total[:, 2 * columns:])
```

```python
import functools
import math

import jax
import jax.numpy as jnp
from jax import lax
from jax.experimental import pallas as pl
from jax.experimental.pallas import tpu as pltpu
from jax.sharding import Mesh, PartitionSpec as P

F32 = jnp.float32
BF16 = jnp.bfloat16
SEED_STEP = 0.4
CHUNK = 256
NT = (((1,), (1,)), ((), ()))
TN = (((0,), (0,)), ((), ()))
NN = (((1,), (0,)), ((), ()))
SWAP = ((0, 1), (1, 0))
STATE_ROWS = 144
MIB = 1 << 20


def dot(a, b, dims):
    return lax.dot_general(a, b, dims, preferred_element_type=F32)


def params(vmem=24, **kw):
    return pltpu.CompilerParams(vmem_limit_bytes=vmem * MIB, **kw)


def cost(flops, nbytes):
    return pl.CostEstimate(flops=flops, bytes_accessed=nbytes, transcendentals=0)


def project_body(idx_ref, own_ref, other_ref, w_ref, out_ref, acc_ref):
    step = pl.program_id(0)
    core = idx_ref[16]
    rows = own_ref.shape[0]

    @pl.when(step == 0)
    def _():
        acc_ref[...] = jnp.zeros_like(acc_ref)

    mine = pl.ds(pl.multiple_of(core * rows, rows), rows)
    theirs = pl.ds(pl.multiple_of((1 - core) * rows, rows), rows)
    w = w_ref[...]
    acc_ref[mine, :] += dot(own_ref[...], w, NN)
    acc_ref[theirs, :] += dot(other_ref[...], w, NN)

    @pl.when(step == pl.num_programs(0) - 1)
    def _():
        out_ref[...] = acc_ref[...].astype(BF16)


def project(idx, own, other, w):
    rows, depth = own.shape
    blocks = 16
    width = depth // blocks
    columns = w.shape[1]
    return pl.pallas_call(
        project_body,
        out_shape=jax.ShapeDtypeStruct((2 * rows, columns), BF16),
        grid_spec=pltpu.PrefetchScalarGridSpec(
            num_scalar_prefetch=1,
            grid=(blocks,),
            in_specs=[
                pl.BlockSpec((rows, width), lambda k, idx: (0, idx[k])),
                pl.BlockSpec((rows, width), lambda k, idx: (0, idx[k])),
                pl.BlockSpec((width, columns), lambda k, idx: (k, 0)),
            ],
            out_specs=pl.BlockSpec((2 * rows, columns), lambda k, idx: (0, 0)),
            scratch_shapes=[pltpu.VMEM((2 * rows, columns), F32)],
        ),
        compiler_params=params(),
        cost_estimate=cost(4 * rows * depth * columns, 4 * rows * depth + 2 * depth * columns),
        name="project",
    )(idx, own, other, w)


def features(rows, seed):
    size = rows.shape[1]
    scale = size ** (-0.25)
    scaled = rows.astype(F32) * scale
    projected = dot(rows, seed, NN) * (SEED_STEP * scale)
    norm = 0.5 * jnp.sum(scaled * scaled, -1, keepdims=True)
    return jnp.exp(projected - norm) * (1.0 / math.sqrt(seed.shape[1]))


def feature_grad(weighted, rows, seed):
    scale = rows.shape[1] ** (-0.25)
    projected = dot(weighted.astype(BF16), seed, NT) * SEED_STEP
    total = jnp.sum(weighted, -1, keepdims=True)
    return (projected - total * (rows.astype(F32) * scale)) * scale


def mask_of(size):
    return lax.broadcasted_iota(jnp.int32, (size, size), 0) >= lax.broadcasted_iota(
        jnp.int32, (size, size), 1
    )


def put_state(ref, head, main, row):
    pad = jnp.zeros((STATE_ROWS - main.shape[0] - 1, main.shape[1]), F32)
    ref[head] = jnp.concatenate([main, row, pad], 0).astype(ref.dtype)


def keys_body(k_ref, v_ref, seed_ref, kf_ref, before_ref, total_ref, carry_ref):
    step = pl.program_id(0)

    @pl.when(step == 0)
    def _():
        carry_ref[...] = jnp.zeros_like(carry_ref)

    before_ref[0] = carry_ref[...]
    for head in range(2):
        cols = slice(128 * head, 128 * head + 128)
        kf = features(k_ref[:, cols], seed_ref[head]).astype(BF16)
        kf_ref[:, 256 * head : 256 * head + 256] = kf
        main = dot(v_ref[:, cols], kf, TN)
        row = jnp.sum(kf.astype(F32), 0, keepdims=True)
        pad = jnp.zeros((STATE_ROWS - 129, 256), F32)
        carry_ref[head] += jnp.concatenate([main, row, pad], 0)

    @pl.when(step == pl.num_programs(0) - 1)
    def _():
        total_ref[...] = carry_ref[...].astype(BF16)


def keys_stage(kvq, seed):
    tok = kvq.shape[0]
    n = tok // CHUNK
    state = (2, STATE_ROWS, 256)
    return pl.pallas_call(
        keys_body,
        grid=(n,),
        in_specs=[
            pl.BlockSpec((CHUNK, 256), lambda i: (i, 0)),
            pl.BlockSpec((CHUNK, 256), lambda i: (i, 1)),
            pl.BlockSpec((2, 128, 256), lambda i: (0, 0, 0)),
        ],
        out_specs=[
            pl.BlockSpec((CHUNK, 512), lambda i: (i, 0)),
            pl.BlockSpec((1,) + state, lambda i: (i, 0, 0, 0)),
            pl.BlockSpec(state, lambda i: (0, 0, 0)),
        ],
        out_shape=[
            jax.ShapeDtypeStruct((tok, 512), BF16),
            jax.ShapeDtypeStruct((n,) + state, F32),
            jax.ShapeDtypeStruct(state, BF16),
        ],
        scratch_shapes=[pltpu.VMEM(state, F32)],
        compiler_params=params(),
        cost_estimate=cost(n * 2 * 4 * 256 * 256 * 128, 4 * MIB),
        name="keys_stage",
    )(kvq, kvq, seed)


def local_body(q_ref, v_ref, kf_ref, seed_ref, before_ref, qf_ref, s_ref, num_ref, den_ref):
    mask = mask_of(CHUNK)
    for head in range(2):
        cols = slice(128 * head, 128 * head + 128)
        wide = slice(256 * head, 256 * head + 256)
        qf = features(q_ref[:, cols], seed_ref[head]).astype(BF16)
        qf_ref[:, wide] = qf
        scores = jnp.where(mask, dot(qf, kf_ref[:, wide], NT), 0.0)
        s16 = scores.astype(BF16)
        s_ref[:, wide] = s16
        main = before_ref[0, head, :128, :].astype(BF16)
        row = before_ref[0, head, 128:129, :]
        num_ref[:, cols] = dot(s16, v_ref[:, cols], NN) + dot(qf, main, NT)
        den_ref[head] = jnp.sum(scores, -1, keepdims=True) + jnp.sum(
            qf.astype(F32) * row, -1, keepdims=True
        )


def local_stage(kvq, kf, seed, before):
    tok = kvq.shape[0]
    n = tok // CHUNK
    return pl.pallas_call(
        local_body,
        grid=(n,),
        in_specs=[
            pl.BlockSpec((CHUNK, 256), lambda i: (i, 2)),
            pl.BlockSpec((CHUNK, 256), lambda i: (i, 1)),
            pl.BlockSpec((CHUNK, 512), lambda i: (i, 0)),
            pl.BlockSpec((2, 128, 256), lambda i: (0, 0, 0)),
            pl.BlockSpec((1, 2, STATE_ROWS, 256), lambda i: (i, 0, 0, 0)),
        ],
        out_specs=[
            pl.BlockSpec((CHUNK, 512), lambda i: (i, 0)),
            pl.BlockSpec((CHUNK, 512), lambda i: (i, 0)),
            pl.BlockSpec((CHUNK, 256), lambda i: (i, 0)),
            pl.BlockSpec((2, CHUNK, 1), lambda i: (0, i, 0)),
        ],
        out_shape=[
            jax.ShapeDtypeStruct((tok, 512), BF16),
            jax.ShapeDtypeStruct((tok, 512), BF16),
            jax.ShapeDtypeStruct((tok, 256), F32),
            jax.ShapeDtypeStruct((2, tok, 1), F32),
        ],
        compiler_params=params(),
        cost_estimate=cost(n * 2 * 10 * 256 * 256 * 128, 6 * MIB),
        name="local_stage",
    )(kvq, kvq, kf, seed, before)


def ratio_body(qf_ref, num_ref, den_ref, g_ref, prefix_ref, gn_ref, gd_ref, total_ref, carry_ref):
    step = pl.program_id(0)

    @pl.when(step == 0)
    def _():
        carry_ref[...] = jnp.zeros_like(carry_ref)

    for head in range(2):
        cols = slice(128 * head, 128 * head + 128)
        wide = slice(256 * head, 256 * head + 256)
        qf = qf_ref[:, wide]
        qf32 = qf.astype(F32)
        main = prefix_ref[head, :128, :].astype(BF16)
        row = prefix_ref[head, 128:129, :]
        num = num_ref[:, cols] + dot(qf, main, NT)
        den = den_ref[head] + jnp.sum(qf32 * row, -1, keepdims=True)
        inverse = 1.0 / den
        g = g_ref[:, cols].astype(F32)
        gn = (g * inverse).astype(BF16)
        gd = -jnp.sum(g * num, -1, keepdims=True) * inverse * inverse
        gn_ref[:, cols] = gn
        gd_ref[head] = gd
        carry_ref[head, :128, :] += dot(gn, qf, TN)
        carry_ref[head, 128:129, :] += jnp.sum(qf32 * gd, 0, keepdims=True)

    @pl.when(step == pl.num_programs(0) - 1)
    def _():
        total_ref[...] = carry_ref[...].astype(BF16)


def ratio_stage(qf, num, den, g, prefix):
    tok = qf.shape[0]
    n = tok // CHUNK
    state = (2, STATE_ROWS, 256)
    return pl.pallas_call(
        ratio_body,
        grid=(n,),
        in_specs=[
            pl.BlockSpec((CHUNK, 512), lambda i: (i, 0)),
            pl.BlockSpec((CHUNK, 256), lambda i: (i, 0)),
            pl.BlockSpec((2, CHUNK, 1), lambda i: (0, i, 0)),
            pl.BlockSpec((CHUNK, 256), lambda i: (i, 0)),
            pl.BlockSpec(state, lambda i: (0, 0, 0)),
        ],
        out_specs=[
            pl.BlockSpec((CHUNK, 256), lambda i: (i, 0)),
            pl.BlockSpec((2, CHUNK, 1), lambda i: (0, i, 0)),
            pl.BlockSpec(state, lambda i: (0, 0, 0)),
        ],
        out_shape=[
            jax.ShapeDtypeStruct((tok, 256), BF16),
            jax.ShapeDtypeStruct((2, tok, 1), F32),
            jax.ShapeDtypeStruct(state, BF16),
        ],
        scratch_shapes=[pltpu.VMEM(state, F32)],
        compiler_params=params(),
        cost_estimate=cost(n * 2 * 4 * 256 * 256 * 128, 4 * MIB),
        name="ratio_stage",
    )(qf, num, den, g, prefix)


def middle_body(
    q_ref, v_ref, kf_ref, qf_ref, s_ref, gn_ref, gd_ref, seed_ref, before_ref, prefix_ref,
    dq_ref, dkf_ref, dv_ref, carry_ref,
):
    step = pl.program_id(0)
    mask = mask_of(CHUNK)

    @pl.when(step == 0)
    def _():
        carry_ref[...] = jnp.zeros_like(carry_ref)

    for head in range(2):
        cols = slice(128 * head, 128 * head + 128)
        wide = slice(256 * head, 256 * head + 256)
        qf, kf, gn, gd = qf_ref[:, wide], kf_ref[:, wide], gn_ref[:, cols], gd_ref[head]
        v = v_ref[:, cols]
        qf32 = qf.astype(F32)
        pairs = jnp.where(mask, dot(gn, v, NT) + gd, 0.0).astype(BF16)
        earlier = prefix_ref[head] + before_ref[0, head]
        main, row = earlier[:128].astype(BF16), earlier[128:129]
        dqf = dot(pairs, kf, NN) + dot(gn, main, NN) + gd * row
        dq_ref[:, cols] = feature_grad(dqf * qf32, q_ref[:, cols], seed_ref[head]).astype(BF16)
        later = carry_ref[head]
        later_main, later_row = later[:128].astype(BF16), later[128:129]
        dkf_ref[:, wide] = dot(pairs, qf, TN) + dot(v, later_main, NN) + later_row
        dv_ref[:, cols] = dot(s_ref[:, wide], gn, TN) + dot(kf, later_main, NT)
        carry_ref[head, :128, :] += dot(gn, qf, TN)
        carry_ref[head, 128:129, :] += jnp.sum(qf32 * gd, 0, keepdims=True)


def middle_stage(kvq, kf, qf, s, gn, gd, seed, before, prefix):
    tok = qf.shape[0]
    n = tok // CHUNK
    state = (2, STATE_ROWS, 256)

    def narrow(column):
        return pl.BlockSpec((CHUNK, 256), lambda i: (n - 1 - i, column))

    wide = pl.BlockSpec((CHUNK, 512), lambda i: (n - 1 - i, 0))
    return pl.pallas_call(
        middle_body,
        grid=(n,),
        in_specs=[
            narrow(2), narrow(1), wide, wide, wide, narrow(0),
            pl.BlockSpec((2, CHUNK, 1), lambda i: (0, n - 1 - i, 0)),
            pl.BlockSpec((2, 128, 256), lambda i: (0, 0, 0)),
            pl.BlockSpec((1,) + state, lambda i: (n - 1 - i, 0, 0, 0)),
            pl.BlockSpec(state, lambda i: (0, 0, 0)),
        ],
        out_specs=[narrow(0), wide, narrow(0)],
        out_shape=[
            jax.ShapeDtypeStruct((tok, 256), BF16),
            jax.ShapeDtypeStruct((tok, 512), F32),
            jax.ShapeDtypeStruct((tok, 256), F32),
        ],
        scratch_shapes=[pltpu.VMEM(state, F32)],
        compiler_params=params(),
        cost_estimate=cost(n * 2 * 20 * 256 * 256 * 128, 10 * MIB),
        name="middle_stage",
    )(kvq, kvq, kf, qf, s, gn, gd, seed, before, prefix)


def last_body(k_ref, v_ref, kf_ref, dkf_ref, dv_ref, seed_ref, suffix_ref, out_ref):
    for head in range(2):
        cols = slice(128 * head, 128 * head + 128)
        wide = slice(256 * head, 256 * head + 256)
        kf = kf_ref[:, wide]
        main = suffix_ref[head, :128, :].astype(BF16)
        row = suffix_ref[head, 128:129, :]
        dkf = dkf_ref[:, wide] + dot(v_ref[:, cols], main, NN) + row
        dk = feature_grad(dkf * kf.astype(F32), k_ref[:, cols], seed_ref[head])
        out_ref[:, cols] = dk.astype(BF16)
        dv = dv_ref[:, cols] + dot(kf, main, NT)
        out_ref[:, 256 + 128 * head : 384 + 128 * head] = dv.astype(BF16)


def last_stage(kvq, kf, dkf, dv, seed, suffix):
    tok = kf.shape[0]
    n = tok // CHUNK
    state = (2, STATE_ROWS, 256)
    return pl.pallas_call(
        last_body,
        grid=(n,),
        in_specs=[
            pl.BlockSpec((CHUNK, 256), lambda i: (i, 0)),
            pl.BlockSpec((CHUNK, 256), lambda i: (i, 1)),
            pl.BlockSpec((CHUNK, 512), lambda i: (i, 0)),
            pl.BlockSpec((CHUNK, 512), lambda i: (i, 0)),
            pl.BlockSpec((CHUNK, 256), lambda i: (i, 0)),
            pl.BlockSpec((2, 128, 256), lambda i: (0, 0, 0)),
            pl.BlockSpec(state, lambda i: (0, 0, 0)),
        ],
        out_specs=pl.BlockSpec((CHUNK, 512), lambda i: (i, 0)),
        out_shape=jax.ShapeDtypeStruct((tok, 512), BF16),
        compiler_params=params(),
        cost_estimate=cost(n * 2 * 6 * 256 * 256 * 128, 6 * MIB),
        name="last_stage",
    )(kvq, kvq, kf, dkf, dv, seed, suffix)


def wgrad_body(idx_ref, own_ref, other_ref, d_ref, out_ref):
    core = idx_ref[16]
    rows = own_ref.shape[0]
    mine = pl.ds(pl.multiple_of(core * rows, rows), rows)
    theirs = pl.ds(pl.multiple_of((1 - core) * rows, rows), rows)
    out = dot(own_ref[...], d_ref[mine, :], TN) + dot(other_ref[...], d_ref[theirs, :], TN)
    out_ref[...] = out.astype(BF16)


def wgrad(idx, own, other, d):
    rows, depth = own.shape
    blocks = 16
    width = depth // blocks
    columns = d.shape[1]
    return pl.pallas_call(
        wgrad_body,
        out_shape=jax.ShapeDtypeStruct((depth, columns), BF16),
        grid_spec=pltpu.PrefetchScalarGridSpec(
            num_scalar_prefetch=1,
            grid=(blocks,),
            in_specs=[
                pl.BlockSpec((rows, width), lambda k, idx: (0, idx[k])),
                pl.BlockSpec((rows, width), lambda k, idx: (0, idx[k])),
                pl.BlockSpec((2 * rows, columns), lambda k, idx: (0, 0)),
            ],
            out_specs=pl.BlockSpec((width, columns), lambda k, idx: (k, 0)),
        ),
        compiler_params=params(),
        cost_estimate=cost(4 * rows * depth * columns, 4 * rows * depth + 2 * depth * columns),
        name="wgrad",
    )(idx, own, other, d)


def back_body(quarter_ref, dm_ref, dt_ref, wm_ref, wt_ref, out_ref):
    out_ref[...] = dot(dm_ref[...], wm_ref[...], NT) + dot(dt_ref[...], wt_ref[...], NT)


def back(quarter, d_mine, d_theirs, w_mine, w_theirs):
    rows, depth = d_mine.shape
    width = 256
    n = w_mine.shape[0] // 4 // width
    return pl.pallas_call(
        back_body,
        out_shape=jax.ShapeDtypeStruct((rows, n * width), F32),
        grid_spec=pltpu.PrefetchScalarGridSpec(
            num_scalar_prefetch=1,
            grid=(n,),
            in_specs=[
                pl.BlockSpec((rows, depth), lambda k, q: (0, 0)),
                pl.BlockSpec((rows, depth), lambda k, q: (0, 0)),
                pl.BlockSpec((width, depth), lambda k, q: (q[0] * n + k, 0)),
                pl.BlockSpec((width, depth), lambda k, q: (q[0] * n + k, 0)),
            ],
            out_specs=pl.BlockSpec((rows, width), lambda k, q: (0, k)),
        ),
        compiler_params=params(),
        cost_estimate=cost(4 * rows * n * width * depth, 8 * MIB),
        name="back",
    )(quarter, d_mine, d_theirs, w_mine, w_theirs)


def swap(a):
    return lax.ppermute(a, "c", SWAP)


def ring(a, axis, by):
    return lax.ppermute(a, axis, [(i, (i + by) % 4) for i in range(4)])


def shift(a, axis, by):
    return lax.ppermute(a, axis, [(i, i + by) for i in range(4) if 0 <= i + by < 4])


def scan_chips(state, direction):
    y = lax.axis_index("y")
    place = y if direction == 1 else 3 - y
    near = [ring(state, "y", direction * by).astype(F32) for by in (1, 2, 3)]
    row_total = (state.astype(F32) + near[0] + near[1] + near[2]).astype(BF16)
    far = [shift(row_total, "z", direction * by).astype(F32) for by in (1, 2, 3)]
    total = far[0] + far[1] + far[2]
    for by in (1, 2, 3):
        total = total + jnp.where(place >= by, near[by - 1], 0.0)
    return total


def in_order(core, mine, theirs, axis=0):
    first = jnp.where(core == 0, mine, theirs)
    second = jnp.where(core == 0, theirs, mine)
    return jnp.concatenate([first, second], axis)


def per_device(tokens, w_query, w_key, w_value, omega_seed, grad_out):
    core = lax.axis_index("c")
    x = lax.axis_index("x")
    rows = tokens.shape[0]

    def heads_of(a, which):
        return lax.dynamic_slice_in_dim(a, which * 256, 256, 1)

    def weights_of(which):
        return jnp.concatenate([heads_of(w, which) for w in (w_key, w_value, w_query)], 1)

    w_chip = in_order(core, weights_of(core), swap(weights_of(1 - core)))
    weights = lax.all_gather(w_chip, ("z", "y"), axis=0, tiled=True)
    other = swap(tokens)
    g = in_order(core, heads_of(grad_out, core), swap(heads_of(grad_out, 1 - core)))
    seed = lax.dynamic_slice_in_dim(omega_seed, 2 * core, 2, 0).astype(BF16)
    idx = jnp.concatenate([jnp.arange(16, dtype=jnp.int32), core.astype(jnp.int32)[None]])

    kvq = project(idx, tokens, other, weights)
    weights_theirs = swap(weights)
    kf, before, total = keys_stage(kvq, seed)
    prefix = scan_chips(total, 1)
    qf, s, num, den = local_stage(kvq, kf, seed, before)
    gn, gd, later = ratio_stage(qf, num, den, g, prefix)
    suffix = scan_chips(later, -1)
    dq, dkf, dv = middle_stage(kvq, kf, qf, s, gn, gd, seed, before, prefix)
    dkv = last_stage(kvq, kf, dkf, dv, seed, suffix)

    d = jnp.concatenate([dkv, dq], 1)

    def tokens_of(a, which):
        return lax.dynamic_slice_in_dim(a, which * rows, rows, 0)

    d_theirs = swap(tokens_of(d, 1 - core))
    d_mine = tokens_of(d, core)

    partial = wgrad(idx, tokens, other, d)
    total_w = lax.psum_scatter(partial, ("z", "y"), scatter_dimension=0, tiled=True)

    def quarter(by):
        where = lax.rem(x + by, 4).astype(jnp.int32)[None]
        return back(where, d_mine, d_theirs, weights, weights_theirs)

    half = rows // 2
    far = quarter(2).astype(BF16)
    from_left = ring(far[:half], "x", 1)
    from_right = ring(far[half:], "x", -1)
    right, left = quarter(1), quarter(3)
    right_plain = ring(right[half:].astype(BF16), "x", 1)
    left_plain = ring(left[:half].astype(BF16), "x", -1)
    right_summed = ring((right[:half] + from_left.astype(F32)).astype(BF16), "x", 1)
    left_summed = ring((left[half:] + from_right.astype(F32)).astype(BF16), "x", -1)
    own = quarter(0)
    top = own[:half] + right_summed.astype(F32) + left_plain.astype(F32)
    bottom = own[half:] + right_plain.astype(F32) + left_summed.astype(F32)
    input_grad = jnp.concatenate([top, bottom], 0).astype(BF16)

    strip = total_w.shape[0] // 2
    keep = lax.dynamic_slice_in_dim(total_w, core * strip, strip, 0)
    give = lax.dynamic_slice_in_dim(total_w, (1 - core) * strip, strip, 0)
    got = swap(give)

    def out(which):
        cols = slice(256 * which, 256 * which + 256)
        return in_order(core, keep[:, cols].astype(F32), got[:, cols].astype(F32), 1)

    return input_grad, out(2), out(0), out(1)


def solution(mesh):
    chips = Mesh(mesh.devices.reshape(4, 4, 2, 4), ("z", "y", "c", "x"))
    seq = ("z", "y", "c")
    placed = (
        P(seq, None),
        P(seq, "x"),
        P(seq, "x"),
        P(seq, "x"),
        P("x", None, None),
        P(seq, "x"),
    )
    return jax.shard_map(
        per_device,
        mesh=chips,
        in_specs=placed,
        out_specs=(P(seq, "x"), P(seq, "x"), P(seq, "x"), P(seq, "x")),
        check_vma=False,
    )
```

```python
import math

import jax
import jax.numpy as jnp
from jax import lax
from jax.experimental import pallas as pl
from jax.experimental.pallas import tpu as pltpu
from jax.sharding import Mesh, PartitionSpec as P


F32 = jnp.float32
BF16 = jnp.bfloat16
SEED_STEP = 0.4
CHUNK = 256
NT = (((1,), (1,)), ((), ()))
TN = (((0,), (0,)), ((), ()))
NN = (((1,), (0,)), ((), ()))
SWAP = ((0, 1), (1, 0))
STATE_ROWS = 144
MIB = 1 << 20


def dot(a, b, dims):
    return lax.dot_general(a, b, dims, preferred_element_type=F32)


GRANT = 12


def params(vmem=GRANT):
    return pltpu.CompilerParams(vmem_limit_bytes=vmem * MIB)


def cost(flops, nbytes):
    return pl.CostEstimate(flops=flops, bytes_accessed=nbytes, transcendentals=0)


def arrange_body(idx_ref, own_ref, other_ref, rows_ref, columns_ref):
    core = idx_ref[16]
    size = own_ref.shape[0]
    mine = pl.ds(pl.multiple_of(core * size, size), size)
    theirs = pl.ds(pl.multiple_of((1 - core) * size, size), size)
    own, other = own_ref[...], other_ref[...]
    rows_ref[mine, :] = own
    rows_ref[theirs, :] = other
    columns_ref[:, mine] = own.T
    columns_ref[:, theirs] = other.T


def arrange(idx, own, other, group):
    size, depth = own.shape
    width = depth // 16
    source = pl.BlockSpec((size, width), lambda k, idx: (0, idx[4 * group + k]))
    return pl.pallas_call(
        arrange_body,
        out_shape=[
            jax.ShapeDtypeStruct((2 * size, 4 * width), BF16),
            jax.ShapeDtypeStruct((4 * width, 2 * size), BF16),
        ],
        grid_spec=pltpu.PrefetchScalarGridSpec(
            num_scalar_prefetch=1,
            grid=(4,),
            in_specs=[source, source],
            out_specs=[
                pl.BlockSpec((2 * size, width), lambda k, idx: (0, k)),
                pl.BlockSpec((width, 2 * size), lambda k, idx: (k, 0)),
            ],
        ),
        compiler_params=params(),
        cost_estimate=cost(4 * MIB, 6 * MIB),
        name="arrange",
    )(idx, own, other)


def halves_dot(x_ref, wa_ref, wb_ref):
    half = wa_ref.shape[0]
    return dot(x_ref[:, :half], wa_ref[...], NN) + dot(x_ref[:, half:], wb_ref[...], NN)


def first_body(x_ref, wa_ref, wb_ref, out_ref):
    out_ref[...] = halves_dot(x_ref, wa_ref, wb_ref)


def more_body(acc_ref, xa_ref, xb_ref, *rest):
    *w_refs, out_ref = rest
    total = acc_ref[...]
    for x_ref, pair in ((xa_ref, w_refs[:2]), (xb_ref, w_refs[2:])):
        total += halves_dot(x_ref, *pair)
    out_ref[...] = total


def end_body(acc_ref, x_ref, wa_ref, wb_ref, out_ref):
    out_ref[...] = (acc_ref[...] + halves_dot(x_ref, wa_ref, wb_ref)).astype(BF16)


def project(body, acc, xs, ws, dtype):
    tok = xs[0].shape[0]
    columns = ws[0].shape[1]
    size = 256

    def tall(a):
        return pl.BlockSpec((size, a.shape[1]), lambda i: (i, 0))

    def whole(a):
        return pl.BlockSpec(a.shape, lambda i: (0, 0))

    ops = acc + xs + ws
    depth = sum(x.shape[1] for x in xs)
    return pl.pallas_call(
        body,
        grid=(tok // size,),
        in_specs=[tall(a) for a in acc + xs] + [whole(w) for w in ws],
        out_specs=pl.BlockSpec((size, columns), lambda i: (i, 0)),
        out_shape=jax.ShapeDtypeStruct((tok, columns), dtype),
        compiler_params=params(16),
        cost_estimate=cost(2 * tok * depth * columns, 8 * MIB),
    )(*ops)


def features(rows, seed):
    size = rows.shape[1]
    scale = size ** (-0.25)
    scaled = rows.astype(F32) * scale
    projected = dot(rows, seed, NN) * (SEED_STEP * scale)
    norm = 0.5 * jnp.sum(scaled * scaled, -1, keepdims=True)
    return jnp.exp(projected - norm) * (1.0 / math.sqrt(seed.shape[1]))


def feature_grad(weighted, rows, seed):
    scale = rows.shape[1] ** (-0.25)
    projected = dot(weighted.astype(BF16), seed, NT) * SEED_STEP
    total = jnp.sum(weighted, -1, keepdims=True)
    return (projected - total * (rows.astype(F32) * scale)) * scale


def mask_of(size):
    return lax.broadcasted_iota(jnp.int32, (size, size), 0) >= lax.broadcasted_iota(
        jnp.int32, (size, size), 1
    )


def keys_body(k_ref, v_ref, seed_ref, kf_ref, before_ref, total_ref, carry_ref):
    step = pl.program_id(0)

    @pl.when(step == 0)
    def _():
        carry_ref[...] = jnp.zeros_like(carry_ref)

    before_ref[0] = carry_ref[...]
    for head in range(2):
        cols = slice(128 * head, 128 * head + 128)
        kf = features(k_ref[:, cols], seed_ref[head]).astype(BF16)
        kf_ref[:, 256 * head : 256 * head + 256] = kf
        main = dot(v_ref[:, cols], kf, TN)
        row = jnp.sum(kf.astype(F32), 0, keepdims=True)
        pad = jnp.zeros((STATE_ROWS - 129, 256), F32)
        carry_ref[head] += jnp.concatenate([main, row, pad], 0)

    @pl.when(step == pl.num_programs(0) - 1)
    def _():
        total_ref[...] = carry_ref[...].astype(BF16)


def keys_stage(kvq, seed):
    tok = kvq.shape[0]
    n = tok // CHUNK
    state = (2, STATE_ROWS, 256)
    return pl.pallas_call(
        keys_body,
        grid=(n,),
        in_specs=[
            pl.BlockSpec((CHUNK, 256), lambda i: (i, 0)),
            pl.BlockSpec((CHUNK, 256), lambda i: (i, 1)),
            pl.BlockSpec((2, 128, 256), lambda i: (0, 0, 0)),
        ],
        out_specs=[
            pl.BlockSpec((CHUNK, 512), lambda i: (i, 0)),
            pl.BlockSpec((1,) + state, lambda i: (i, 0, 0, 0)),
            pl.BlockSpec(state, lambda i: (0, 0, 0)),
        ],
        out_shape=[
            jax.ShapeDtypeStruct((tok, 512), BF16),
            jax.ShapeDtypeStruct((n,) + state, F32),
            jax.ShapeDtypeStruct(state, BF16),
        ],
        scratch_shapes=[pltpu.VMEM(state, F32)],
        compiler_params=params(),
        cost_estimate=cost(n * 2 * 4 * 256 * 256 * 128, 4 * MIB),
        name="keys_stage",
    )(kvq, kvq, seed)


def local_body(q_ref, v_ref, kf_ref, seed_ref, before_ref, qf_ref, s_ref, num_ref, den_ref):
    mask = mask_of(CHUNK)
    for head in range(2):
        cols = slice(128 * head, 128 * head + 128)
        wide = slice(256 * head, 256 * head + 256)
        qf = features(q_ref[:, cols], seed_ref[head]).astype(BF16)
        qf_ref[:, wide] = qf
        scores = jnp.where(mask, dot(qf, kf_ref[:, wide], NT), 0.0)
        s16 = scores.astype(BF16)
        s_ref[:, wide] = s16
        main = before_ref[0, head, :128, :].astype(BF16)
        row = before_ref[0, head, 128:129, :]
        num_ref[:, cols] = dot(s16, v_ref[:, cols], NN) + dot(qf, main, NT)
        den_ref[head] = jnp.sum(scores, -1, keepdims=True) + jnp.sum(
            qf.astype(F32) * row, -1, keepdims=True
        )


def local_stage(kvq, kf, seed, before):
    tok = kvq.shape[0]
    n = tok // CHUNK
    return pl.pallas_call(
        local_body,
        grid=(n,),
        in_specs=[
            pl.BlockSpec((CHUNK, 256), lambda i: (i, 2)),
            pl.BlockSpec((CHUNK, 256), lambda i: (i, 1)),
            pl.BlockSpec((CHUNK, 512), lambda i: (i, 0)),
            pl.BlockSpec((2, 128, 256), lambda i: (0, 0, 0)),
            pl.BlockSpec((1, 2, STATE_ROWS, 256), lambda i: (i, 0, 0, 0)),
        ],
        out_specs=[
            pl.BlockSpec((CHUNK, 512), lambda i: (i, 0)),
            pl.BlockSpec((CHUNK, 512), lambda i: (i, 0)),
            pl.BlockSpec((CHUNK, 256), lambda i: (i, 0)),
            pl.BlockSpec((2, CHUNK, 1), lambda i: (0, i, 0)),
        ],
        out_shape=[
            jax.ShapeDtypeStruct((tok, 512), BF16),
            jax.ShapeDtypeStruct((tok, 512), BF16),
            jax.ShapeDtypeStruct((tok, 256), F32),
            jax.ShapeDtypeStruct((2, tok, 1), F32),
        ],
        compiler_params=params(),
        cost_estimate=cost(n * 2 * 10 * 256 * 256 * 128, 6 * MIB),
        name="local_stage",
    )(kvq, kvq, kf, seed, before)


def ratio_body(qf_ref, num_ref, den_ref, g_ref, prefix_ref, gn_ref, gd_ref, total_ref, carry_ref):
    step = pl.program_id(0)

    @pl.when(step == 0)
    def _():
        carry_ref[...] = jnp.zeros_like(carry_ref)

    for head in range(2):
        cols = slice(128 * head, 128 * head + 128)
        wide = slice(256 * head, 256 * head + 256)
        qf = qf_ref[:, wide]
        qf32 = qf.astype(F32)
        main = prefix_ref[head, :128, :].astype(BF16)
        row = prefix_ref[head, 128:129, :]
        num = num_ref[:, cols] + dot(qf, main, NT)
        den = den_ref[head] + jnp.sum(qf32 * row, -1, keepdims=True)
        inverse = 1.0 / den
        g = g_ref[:, cols].astype(F32)
        gn = (g * inverse).astype(BF16)
        gd = -jnp.sum(g * num, -1, keepdims=True) * inverse * inverse
        gn_ref[:, cols] = gn
        gd_ref[head] = gd
        carry_ref[head, :128, :] += dot(gn, qf, TN)
        carry_ref[head, 128:129, :] += jnp.sum(qf32 * gd, 0, keepdims=True)

    @pl.when(step == pl.num_programs(0) - 1)
    def _():
        total_ref[...] = carry_ref[...].astype(BF16)


def ratio_stage(qf, num, den, g, prefix):
    tok = qf.shape[0]
    n = tok // CHUNK
    state = (2, STATE_ROWS, 256)
    return pl.pallas_call(
        ratio_body,
        grid=(n,),
        in_specs=[
            pl.BlockSpec((CHUNK, 512), lambda i: (i, 0)),
            pl.BlockSpec((CHUNK, 256), lambda i: (i, 0)),
            pl.BlockSpec((2, CHUNK, 1), lambda i: (0, i, 0)),
            pl.BlockSpec((CHUNK, 256), lambda i: (i, 0)),
            pl.BlockSpec(state, lambda i: (0, 0, 0)),
        ],
        out_specs=[
            pl.BlockSpec((CHUNK, 256), lambda i: (i, 0)),
            pl.BlockSpec((2, CHUNK, 1), lambda i: (0, i, 0)),
            pl.BlockSpec(state, lambda i: (0, 0, 0)),
        ],
        out_shape=[
            jax.ShapeDtypeStruct((tok, 256), BF16),
            jax.ShapeDtypeStruct((2, tok, 1), F32),
            jax.ShapeDtypeStruct(state, BF16),
        ],
        scratch_shapes=[pltpu.VMEM(state, F32)],
        compiler_params=params(),
        cost_estimate=cost(n * 2 * 4 * 256 * 256 * 128, 4 * MIB),
        name="ratio_stage",
    )(qf, num, den, g, prefix)


def middle_body(
    q_ref, v_ref, kf_ref, qf_ref, s_ref, gn_ref, gd_ref, seed_ref, before_ref, prefix_ref,
    dq_ref, dqt_ref, dkf_ref, dv_ref, carry_ref,
):
    step = pl.program_id(0)
    mask = mask_of(CHUNK)

    @pl.when(step == 0)
    def _():
        carry_ref[...] = jnp.zeros_like(carry_ref)

    for head in range(2):
        cols = slice(128 * head, 128 * head + 128)
        wide = slice(256 * head, 256 * head + 256)
        qf, kf, gn, gd = qf_ref[:, wide], kf_ref[:, wide], gn_ref[:, cols], gd_ref[head]
        v = v_ref[:, cols]
        qf32 = qf.astype(F32)
        pairs = jnp.where(mask, dot(gn, v, NT) + gd, 0.0).astype(BF16)
        earlier = prefix_ref[head] + before_ref[0, head]
        main, row = earlier[:128].astype(BF16), earlier[128:129]
        dqf = dot(pairs, kf, NN) + dot(gn, main, NN) + gd * row
        dq = feature_grad(dqf * qf32, q_ref[:, cols], seed_ref[head]).astype(BF16)
        dq_ref[:, cols] = dq
        dqt_ref[cols, :] = dq.T
        later = carry_ref[head]
        later_main, later_row = later[:128].astype(BF16), later[128:129]
        dkf_ref[:, wide] = dot(pairs, qf, TN) + dot(v, later_main, NN) + later_row
        dv_ref[:, cols] = dot(s_ref[:, wide], gn, TN) + dot(kf, later_main, NT)
        carry_ref[head, :128, :] += dot(gn, qf, TN)
        carry_ref[head, 128:129, :] += jnp.sum(qf32 * gd, 0, keepdims=True)


def middle_stage(kvq, kf, qf, s, gn, gd, seed, before, prefix):
    tok = qf.shape[0]
    n = tok // CHUNK
    state = (2, STATE_ROWS, 256)

    def narrow(column):
        return pl.BlockSpec((CHUNK, 256), lambda i: (n - 1 - i, column))

    wide = pl.BlockSpec((CHUNK, 512), lambda i: (n - 1 - i, 0))
    return pl.pallas_call(
        middle_body,
        grid=(n,),
        in_specs=[
            narrow(2), narrow(1), wide, wide, wide, narrow(0),
            pl.BlockSpec((2, CHUNK, 1), lambda i: (0, n - 1 - i, 0)),
            pl.BlockSpec((2, 128, 256), lambda i: (0, 0, 0)),
            pl.BlockSpec((1,) + state, lambda i: (n - 1 - i, 0, 0, 0)),
            pl.BlockSpec(state, lambda i: (0, 0, 0)),
        ],
        out_specs=[
            narrow(0),
            pl.BlockSpec((256, CHUNK), lambda i: (0, n - 1 - i)),
            wide,
            narrow(0),
        ],
        out_shape=[
            jax.ShapeDtypeStruct((tok, 256), BF16),
            jax.ShapeDtypeStruct((256, tok), BF16),
            jax.ShapeDtypeStruct((tok, 512), F32),
            jax.ShapeDtypeStruct((tok, 256), F32),
        ],
        scratch_shapes=[pltpu.VMEM(state, F32)],
        compiler_params=params(),
        cost_estimate=cost(n * 2 * 20 * 256 * 256 * 128, 10 * MIB),
        name="middle_stage",
    )(kvq, kvq, kf, qf, s, gn, gd, seed, before, prefix)


def last_body(k_ref, v_ref, kf_ref, dkf_ref, dv_ref, seed_ref, suffix_ref, out_ref, outt_ref):
    for head in range(2):
        cols = slice(128 * head, 128 * head + 128)
        wide = slice(256 * head, 256 * head + 256)
        kf = kf_ref[:, wide]
        main = suffix_ref[head, :128, :].astype(BF16)
        row = suffix_ref[head, 128:129, :]
        dkf = dkf_ref[:, wide] + dot(v_ref[:, cols], main, NN) + row
        dk = feature_grad(dkf * kf.astype(F32), k_ref[:, cols], seed_ref[head]).astype(BF16)
        dv = (dv_ref[:, cols] + dot(kf, main, NT)).astype(BF16)
        dv_cols = slice(256 + 128 * head, 384 + 128 * head)
        out_ref[:, cols] = dk
        out_ref[:, dv_cols] = dv
        outt_ref[cols, :] = dk.T
        outt_ref[dv_cols, :] = dv.T


def last_stage(kvq, kf, dkf, dv, seed, suffix):
    tok = kf.shape[0]
    n = tok // CHUNK
    state = (2, STATE_ROWS, 256)
    return pl.pallas_call(
        last_body,
        grid=(n,),
        in_specs=[
            pl.BlockSpec((CHUNK, 256), lambda i: (i, 0)),
            pl.BlockSpec((CHUNK, 256), lambda i: (i, 1)),
            pl.BlockSpec((CHUNK, 512), lambda i: (i, 0)),
            pl.BlockSpec((CHUNK, 512), lambda i: (i, 0)),
            pl.BlockSpec((CHUNK, 256), lambda i: (i, 0)),
            pl.BlockSpec((2, 128, 256), lambda i: (0, 0, 0)),
            pl.BlockSpec(state, lambda i: (0, 0, 0)),
        ],
        out_specs=[
            pl.BlockSpec((CHUNK, 512), lambda i: (i, 0)),
            pl.BlockSpec((512, CHUNK), lambda i: (0, i)),
        ],
        out_shape=[
            jax.ShapeDtypeStruct((tok, 512), BF16),
            jax.ShapeDtypeStruct((512, tok), BF16),
        ],
        compiler_params=params(),
        cost_estimate=cost(n * 2 * 6 * 256 * 256 * 128, 6 * MIB),
        name="last_stage",
    )(kvq, kvq, kf, dkf, dv, seed, suffix)


def wgrad_body(x_ref, dkv_ref, dq_ref, out_ref):
    x = x_ref[...]
    out_ref[:, :512] = dot(x, dkv_ref[...], NN)
    out_ref[:, 512:] = dot(x, dq_ref[...], NN)


def wgrad(x, dkv, dq):
    depth, tok = x.shape
    columns = dkv.shape[1] + dq.shape[1]
    size = 256
    return pl.pallas_call(
        wgrad_body,
        grid=(depth // size,),
        in_specs=[
            pl.BlockSpec((size, tok), lambda i: (i, 0)),
            pl.BlockSpec(dkv.shape, lambda i: (0, 0)),
            pl.BlockSpec(dq.shape, lambda i: (0, 0)),
        ],
        out_specs=pl.BlockSpec((size, columns), lambda i: (i, 0)),
        out_shape=jax.ShapeDtypeStruct((depth, columns), F32),
        compiler_params=params(),
        cost_estimate=cost(2 * tok * depth * columns, 6 * MIB),
        name="wgrad",
    )(x, dkv, dq)


def finish_body(core_ref, keep_ref, got_ref, q_ref, k_ref, v_ref):
    core = core_ref[0]
    mine = pl.ds(pl.multiple_of(core * 256, 256), 256)
    theirs = pl.ds(pl.multiple_of((1 - core) * 256, 256), 256)
    for place, ref in enumerate((k_ref, v_ref, q_ref)):
        cols = slice(256 * place, 256 * place + 256)
        ref[:, mine] = keep_ref[:, cols].astype(F32)
        ref[:, theirs] = got_ref[:, cols].astype(F32)


def finish(core, keep, got):
    rows = keep.shape[0]
    out = jax.ShapeDtypeStruct((rows, 512), F32)
    whole = pl.BlockSpec(keep.shape, lambda i, core: (0, 0))
    return pl.pallas_call(
        finish_body,
        out_shape=[out] * 3,
        grid_spec=pltpu.PrefetchScalarGridSpec(
            num_scalar_prefetch=1,
            grid=(1,),
            in_specs=[whole, whole],
            out_specs=[pl.BlockSpec((rows, 512), lambda i, core: (0, 0))] * 3,
        ),
        compiler_params=params(8),
        cost_estimate=cost(MIB, MIB),
        name="finish",
    )(core, keep, got)


def collect_body(place_ref, *refs):
    *pieces, out_ref, sems = refs
    size = pieces[0].shape[0] // 2
    copies = []
    for slot in range(2 * len(pieces)):
        to = pl.ds(pl.multiple_of(place_ref[slot] * size, size), size)
        source = pieces[slot // 2].at[pl.ds(slot % 2 * size, size), :]
        copies.append(pltpu.make_async_copy(source, out_ref.at[to, :], sems.at[slot]))
    for copy in copies:
        copy.start()
    for copy in copies:
        copy.wait()


def collect(place, pieces):
    rows, columns = pieces[0].shape
    n = len(pieces)
    return pl.pallas_call(
        collect_body,
        out_shape=jax.ShapeDtypeStruct((n * rows, columns), BF16),
        grid_spec=pltpu.PrefetchScalarGridSpec(
            num_scalar_prefetch=1,
            grid=(1,),
            in_specs=[pl.BlockSpec((rows, columns), lambda i, place: (0, 0))] * n,
            out_specs=pl.BlockSpec(memory_space=pl.ANY),
            scratch_shapes=[pltpu.SemaphoreType.DMA((2 * n,))],
        ),
        compiler_params=params(16),
        cost_estimate=cost(MIB, 12 * MIB),
        name="collect",
    )(place, *pieces)


def back_body(place_ref, mkv_ref, mq_ref, tkv_ref, tq_ref, wm_ref, wt_ref, out_ref):
    out_ref[...] = (
        dot(wm_ref[:, :512], mkv_ref[...], NN)
        + dot(wm_ref[:, 512:], mq_ref[...], NN)
        + dot(wt_ref[:, :512], tkv_ref[...], NN)
        + dot(wt_ref[:, 512:], tq_ref[...], NN)
    )


def back(place, dkvt, dqt, theirs_kv, theirs_q, w_mine, w_theirs):
    rows = theirs_kv.shape[1]
    depth = w_mine.shape[1]
    width = 512
    n = place.shape[0] - 1

    def half_of(a):
        return pl.BlockSpec((a.shape[0], rows), lambda k, p: (0, p[0]))

    def whole(a):
        return pl.BlockSpec(a.shape, lambda k, p: (0, 0))

    weights = pl.BlockSpec((width, depth), lambda k, p: (p[1 + k], 0))
    return pl.pallas_call(
        back_body,
        out_shape=jax.ShapeDtypeStruct((n * width, rows), F32),
        grid_spec=pltpu.PrefetchScalarGridSpec(
            num_scalar_prefetch=1,
            grid=(n,),
            in_specs=[
                half_of(dkvt), half_of(dqt), whole(theirs_kv), whole(theirs_q), weights, weights,
            ],
            out_specs=pl.BlockSpec((width, rows), lambda k, p: (k, 0)),
        ),
        compiler_params=params(),
        cost_estimate=cost(4 * rows * n * width * depth, 8 * MIB),
        name="back",
    )(place, dkvt, dqt, theirs_kv, theirs_q, w_mine, w_theirs)


def turn_body(own_ref, at_ref, ab_ref, bt_ref, bb_ref, out_ref):
    upper = pl.program_id(0) < pl.num_programs(0) // 2
    after = jnp.where(upper, at_ref[...].astype(F32), ab_ref[...].astype(F32))
    before = jnp.where(upper, bt_ref[...].astype(F32), bb_ref[...].astype(F32))
    out_ref[...] = (own_ref[...] + after + before).astype(BF16).T


def turn(own, after, before):
    columns, rows = own.shape
    size = 256
    n = columns // size
    part = pl.BlockSpec((size, rows), lambda i: (i, 0))
    top = pl.BlockSpec((size, rows), lambda i: (jnp.minimum(i, n // 2 - 1), 0))
    bottom = pl.BlockSpec((size, rows), lambda i: (jnp.maximum(i - n // 2, 0), 0))
    return pl.pallas_call(
        turn_body,
        grid=(n,),
        in_specs=[part, top, bottom, top, bottom],
        out_specs=pl.BlockSpec((rows, size), lambda i: (0, i)),
        out_shape=jax.ShapeDtypeStruct((rows, columns), BF16),
        compiler_params=params(),
        cost_estimate=cost(4 * MIB, 6 * MIB),
        name="turn",
    )(own, *after, *before)


def swap(a):
    return lax.ppermute(a, "c", SWAP)


def ring(a, axis, by):
    return lax.ppermute(a, axis, [(i, (i + by) % 4) for i in range(4)])


def along(a, by, inner):
    pairs = []
    for z in range(4):
        for y in range(4):
            for c in range(2):
                over_y = (c == 0) == inner
                to = (z, (y + by) % 4) if over_y else ((z + by) % 4, y)
                pairs.append(((z * 4 + y) * 2 + c, (to[0] * 4 + to[1]) * 2 + c))
    return lax.ppermute(a, ("z", "y", "c"), pairs)


def gather_ring(a):
    half = a.shape[0] // 2
    before = along(a, 1, True)
    after = along(a, -1, True)
    top = along(before[:half], 1, True)
    bottom = along(after[half:], -1, True)
    return a, after, top, bottom, before


def gather_halves(top, bottom):
    top3 = along(top, 1, False)
    bottom1 = along(bottom, -1, False)
    bottom3 = along(bottom, 1, False)
    top1 = along(top, -1, False)
    top2 = along(top3, 1, False)
    bottom2 = along(bottom1, -1, False)
    return (top, bottom), (top1, bottom1), (top2, bottom2), (top3, bottom3)


def scatter_ring(far, after, before, send):
    far = far.astype(BF16)
    half = far.shape[0] // 2
    top = send(far[:half], 1).astype(F32)
    bottom = send(far[half:], -1).astype(F32)
    after_plain = send(after[half:].astype(BF16), 1)
    before_plain = send(before[:half].astype(BF16), -1)
    after_sum = send((after[:half] + top).astype(BF16), 1)
    before_sum = send((before[half:] + bottom).astype(BF16), -1)
    return (after_sum, after_plain), (before_plain, before_sum)


def scatter_small(part):
    far = part(2).astype(BF16)
    half = far.shape[0] // 2
    top = along(far[:half], 1, True).astype(F32)
    bottom = along(far[half:], -1, True).astype(F32)
    after, before = part(1), part(3)
    after = jnp.concatenate([after[:half] + top, after[half:]], 0).astype(BF16)
    before = jnp.concatenate([before[:half], before[half:] + bottom], 0).astype(BF16)
    after = along(after, 1, True).astype(F32)
    before = along(before, -1, True).astype(F32)
    return part(0) + after + before


def scan_flags(inner, outer, direction):
    inner = inner if direction == 1 else 3 - inner
    outer = outer if direction == 1 else 3 - outer
    return tuple((inner >= by, outer + by > 3) for by in (1, 3, 2))


def scan_chips(state, first, flags, direction):
    near = [along(state, direction * by, True).astype(F32) for by in (1, 3, 2)]
    own = state.astype(F32)
    ahead = jnp.zeros_like(own)
    for (passed, _), a in zip(flags, near):
        ahead = ahead + jnp.where(passed, a, 0.0)
    every = near[0] + near[1] + near[2] + own
    straight = jnp.where(first, every, ahead + own).astype(BF16)
    wrapped = jnp.where(first, 0.0, ahead).astype(BF16)
    total = ahead
    for by, (_, wraps) in zip((1, 3, 2), flags):
        message = jnp.where(wraps, wrapped, straight)
        total = total + along(message, direction * by, False).astype(F32)
    return total


def in_order(first, mine, theirs, axis=0):
    one = jnp.where(first, mine, theirs)
    two = jnp.where(first, theirs, mine)
    return jnp.concatenate([one, two], axis)


def half_of(first, a, axis):
    size = a.shape[axis] // 2
    low = lax.slice_in_dim(a, 0, size, axis=axis)
    high = lax.slice_in_dim(a, size, 2 * size, axis=axis)
    return jnp.where(first, low, high), jnp.where(first, high, low)


def per_device(tokens, w_query, w_key, w_value, omega_seed, grad_out):
    core, x, y, z = (lax.axis_index(name).astype(jnp.int32) for name in ("c", "x", "y", "z"))
    outer, inner = jnp.where(core == 0, z, y), jnp.where(core == 0, y, z)
    step = jnp.arange(4, dtype=jnp.int32)
    along_outer, along_inner = (outer + step) % 4, (inner + step) % 4
    chip = jnp.where(
        core == 0,
        along_outer[:, None] * 4 + along_inner[None, :],
        along_inner[None, :] * 4 + along_outer[:, None],
    ).reshape(16)

    def place_of(*steps):
        rows = [2 * lax.rem(x + by, 4) + i for by in steps for i in range(2)]
        return jnp.stack([core] + rows)

    where = (
        core == 0,
        jnp.concatenate([chip, core[None]]),
        chip,
        core[None],
        place_of(2),
        place_of(1, 3),
        place_of(0),
        scan_flags(inner, outer, 1),
        scan_flags(inner, outer, -1),
    )
    where, tokens, w_query, w_key, w_value, omega_seed, grad_out = lax.optimization_barrier(
        (where, tokens, w_query, w_key, w_value, omega_seed, grad_out)
    )
    first, idx, chip, core, far_place, side_place, own_place, ahead_flags, behind_flags = where

    def heads_of(*arrays):
        pairs = [half_of(first, a, 1) for a in arrays]
        return [jnp.concatenate([p[i] for p in pairs], 1) for i in range(2)]

    w_mine, w_give = heads_of(w_key, w_value, w_query)
    w_got = swap(w_give)
    w_chip = in_order(first, w_mine, w_got)
    g_mine, g_give = heads_of(grad_out)
    g_give, _ = lax.optimization_barrier((g_give, w_got))
    g_got = swap(g_give)
    g = in_order(first, g_mine, g_got)
    tokens_late, _ = lax.optimization_barrier((tokens, g_got))
    other = swap(tokens_late)
    seed = half_of(first, omega_seed, 0)[0].astype(BF16)

    w0, w1, w2_top, w2_bottom, w3 = gather_ring(w_chip)
    w_groups = gather_halves(
        jnp.concatenate([w0, w1], 0), jnp.concatenate([w2_top, w2_bottom, w3], 0)
    )
    arranged = [arrange(idx, tokens, other, a) for a in range(4)]
    xs = [a[0] for a in arranged]
    acc = project(first_body, [], [xs[0]], list(w_groups[0]), F32)
    pieces = list(w_groups[1] + w_groups[3])
    acc = project(more_body, [acc], [xs[1], xs[3]], pieces, F32)
    kvq = project(end_body, [acc], [xs[2]], list(w_groups[2]), BF16)

    kf, before, total = keys_stage(kvq, seed)
    prefix = scan_chips(total, first, ahead_flags, 1)
    weights = collect(chip, [p for pair in w_groups for p in pair])
    weights_theirs = swap(weights)
    qf, s, num, den = local_stage(kvq, kf, seed, before)
    gn, gd, later = ratio_stage(qf, num, den, g, prefix)
    suffix = scan_chips(later, first, behind_flags, -1)
    dq, dqt, dkf, dv = middle_stage(kvq, kf, qf, s, gn, gd, seed, before, prefix)
    dkv, dkvt = last_stage(kvq, kf, dkf, dv, seed, suffix)

    theirs_q = swap(half_of(first, dqt, 1)[1])
    theirs_kv = swap(half_of(first, dkvt, 1)[1])

    def group(a):
        return wgrad(arranged[a][1], dkv, dq)

    def quarters(place):
        return back(place, dkvt, dqt, theirs_kv, theirs_q, weights, weights_theirs)

    after, before = scatter_ring(group(2), group(1), group(3), lambda a, by: along(a, by, False))
    own = group(0)
    half = own.shape[0] // 2
    row_sum = [
        own[i * half : (i + 1) * half] + after[i].astype(F32) + before[i].astype(F32)
        for i in range(2)
    ]

    def strip_of(b):
        size = half // 2
        return row_sum[b // 2][b % 2 * size : (b % 2 + 1) * size]

    total_w = scatter_small(strip_of).astype(BF16)

    sides = quarters(side_place)
    columns = sides.shape[0] // 2
    after, before = scatter_ring(
        quarters(far_place), sides[:columns], sides[columns:], lambda a, by: ring(a, "x", by)
    )
    input_grad = turn(quarters(own_place), after, before)

    keep, give = half_of(first, total_w, 0)
    return input_grad, *finish(core, keep, swap(give))


def solution(mesh):
    chips = Mesh(mesh.devices.reshape(4, 4, 2, 4), ("z", "y", "c", "x"))
    seq = ("z", "y", "c")
    placed = (
        P(seq, None),
        P(seq, "x"),
        P(seq, "x"),
        P(seq, "x"),
        P("x", None, None),
        P(seq, "x"),
    )
    specs = (P(seq, "x"), P(seq, "x"), P(seq, "x"), P(seq, "x"))

    return jax.shard_map(per_device, mesh=chips, in_specs=placed, out_specs=specs, check_vma=False)
```

```python
import math

import jax
import jax.numpy as jnp
from jax import lax
from jax.experimental import pallas as pl
from jax.experimental.pallas import tpu as pltpu
from jax.sharding import Mesh, PartitionSpec as P


F32 = jnp.float32
BF16 = jnp.bfloat16
SEED_STEP = 0.4
CHUNK = 256
NT = (((1,), (1,)), ((), ()))
TN = (((0,), (0,)), ((), ()))
NN = (((1,), (0,)), ((), ()))
SWAP = ((0, 1), (1, 0))
STATE_ROWS = 144
MIB = 1 << 20


def dot(a, b, dims):
    return lax.dot_general(a, b, dims, preferred_element_type=F32)


GRANT = 12


def params(vmem=GRANT):
    return pltpu.CompilerParams(vmem_limit_bytes=vmem * MIB)


def cost(flops, nbytes):
    return pl.CostEstimate(flops=flops, bytes_accessed=nbytes, transcendentals=0)


def halve_body(core_ref, *refs):
    *sources, mine_ref, give_ref = refs
    core = core_ref[0]
    half = sources[0].shape[1] // 2
    mine = pl.ds(pl.multiple_of(core * half, half), half)
    give = pl.ds(pl.multiple_of((1 - core) * half, half), half)
    for i, ref in enumerate(sources):
        cols = slice(half * i, half * i + half)
        mine_ref[:, cols] = ref[:, mine]
        give_ref[:, cols] = ref[:, give]


def halve(core, sources):
    size, columns = sources[0].shape
    whole = pl.BlockSpec((size, columns), lambda i, core: (0, 0))
    shape = (size, len(sources) * columns // 2)
    return pl.pallas_call(
        halve_body,
        out_shape=[jax.ShapeDtypeStruct(shape, BF16)] * 2,
        grid_spec=pltpu.PrefetchScalarGridSpec(
            num_scalar_prefetch=1,
            grid=(1,),
            in_specs=[whole] * len(sources),
            out_specs=[pl.BlockSpec(shape, lambda i, core: (0, 0))] * 2,
        ),
        compiler_params=params(56),
        cost_estimate=cost(MIB, MIB),
        name="halve",
    )(core, *sources)


def arrange_body(idx_ref, own_ref, other_ref, rows_ref, columns_ref):
    core = idx_ref[16]
    size = own_ref.shape[0]
    mine = pl.ds(pl.multiple_of(core * size, size), size)
    theirs = pl.ds(pl.multiple_of((1 - core) * size, size), size)
    own, other = own_ref[...], other_ref[...]
    rows_ref[mine, :] = own
    rows_ref[theirs, :] = other
    columns_ref[:, mine] = own.T
    columns_ref[:, theirs] = other.T


def arrange(idx, own, other, group):
    size, depth = own.shape
    width = depth // 16
    source = pl.BlockSpec((size, width), lambda k, idx: (0, idx[4 * group + k]))
    return pl.pallas_call(
        arrange_body,
        out_shape=[
            jax.ShapeDtypeStruct((2 * size, 4 * width), BF16),
            jax.ShapeDtypeStruct((4 * width, 2 * size), BF16),
        ],
        grid_spec=pltpu.PrefetchScalarGridSpec(
            num_scalar_prefetch=1,
            grid=(4,),
            in_specs=[source, source],
            out_specs=[
                pl.BlockSpec((2 * size, width), lambda k, idx: (0, k)),
                pl.BlockSpec((width, 2 * size), lambda k, idx: (k, 0)),
            ],
        ),
        compiler_params=params(),
        cost_estimate=cost(4 * MIB, 6 * MIB),
        name="arrange",
    )(idx, own, other)


def halves_dot(x_ref, wa_ref, wb_ref):
    half = wa_ref.shape[0]
    return dot(x_ref[:, :half], wa_ref[...], NN) + dot(x_ref[:, half:], wb_ref[...], NN)


def first_body(x_ref, wa_ref, wb_ref, out_ref):
    out_ref[...] = halves_dot(x_ref, wa_ref, wb_ref)


def more_body(acc_ref, xa_ref, xb_ref, *rest):
    *w_refs, out_ref = rest
    total = acc_ref[...]
    for x_ref, pair in ((xa_ref, w_refs[:2]), (xb_ref, w_refs[2:])):
        total += halves_dot(x_ref, *pair)
    out_ref[...] = total


def top_body(acc_ref, x_ref, w_ref, out_ref):
    out_ref[...] = acc_ref[...] + dot(x_ref[:, : w_ref.shape[0]], w_ref[...], NN)


def end_body(acc_ref, x_ref, w_ref, out_ref):
    out = acc_ref[...] + dot(x_ref[:, w_ref.shape[0] :], w_ref[...], NN)
    out_ref[...] = out.astype(BF16)


def project(body, acc, xs, ws, dtype):
    tok = xs[0].shape[0]
    columns = ws[0].shape[1]
    size = 256

    def tall(a):
        return pl.BlockSpec((size, a.shape[1]), lambda i: (i, 0))

    def whole(a):
        return pl.BlockSpec(a.shape, lambda i: (0, 0))

    ops = acc + xs + ws
    depth = sum(x.shape[1] for x in xs)
    return pl.pallas_call(
        body,
        grid=(tok // size,),
        in_specs=[tall(a) for a in acc + xs] + [whole(w) for w in ws],
        out_specs=pl.BlockSpec((size, columns), lambda i: (i, 0)),
        out_shape=jax.ShapeDtypeStruct((tok, columns), dtype),
        compiler_params=params(16),
        cost_estimate=cost(2 * tok * depth * columns, 8 * MIB),
    )(*ops)


def features(rows, seed):
    size = rows.shape[1]
    scale = size ** (-0.25)
    scaled = rows.astype(F32) * scale
    projected = dot(rows, seed, NN) * (SEED_STEP * scale)
    norm = 0.5 * jnp.sum(scaled * scaled, -1, keepdims=True)
    return jnp.exp(projected - norm) * (1.0 / math.sqrt(seed.shape[1]))


def feature_grad(weighted, rows, seed):
    scale = rows.shape[1] ** (-0.25)
    projected = dot(weighted.astype(BF16), seed, NT) * SEED_STEP
    total = jnp.sum(weighted, -1, keepdims=True)
    return (projected - total * (rows.astype(F32) * scale)) * scale


def mask_of(size):
    return lax.broadcasted_iota(jnp.int32, (size, size), 0) >= lax.broadcasted_iota(
        jnp.int32, (size, size), 1
    )


PER_STEP = 2


VMEM = pl.BlockSpec(memory_space=pltpu.VMEM)


def over_chunks(n, body):
    def step(i, _):
        for part in range(PER_STEP):
            start = (i * PER_STEP + part) * CHUNK
            body(i * PER_STEP + part, pl.ds(pl.multiple_of(start, CHUNK), CHUNK))

    lax.fori_loop(0, n // PER_STEP, step, None)


def keys_body(kvq_ref, seed_ref, kf_ref, before_ref, total_ref, carry_ref):
    carry_ref[...] = jnp.zeros_like(carry_ref)
    pad = jnp.zeros((STATE_ROWS - 129, 256), F32)

    def chunk(i, rows):
        for head in range(2):
            state = carry_ref[head]
            before_ref[i, head] = state
            kf = features(kvq_ref[rows, 128 * head : 128 * head + 128], seed_ref[head])
            kf = kf.astype(BF16)
            kf_ref[rows, 256 * head : 256 * head + 256] = kf
            main = dot(kvq_ref[rows, 256 + 128 * head : 384 + 128 * head], kf, TN)
            row = jnp.sum(kf.astype(F32), 0, keepdims=True)
            carry_ref[head] = state + jnp.concatenate([main, row, pad], 0)

    over_chunks(kvq_ref.shape[0] // CHUNK, chunk)
    total_ref[...] = carry_ref[...].astype(BF16)


def keys_stage(kvq, seed):
    tok = kvq.shape[0]
    n = tok // CHUNK
    state = (2, STATE_ROWS, 256)
    return pl.pallas_call(
        keys_body,
        in_specs=[VMEM] * 2,
        out_specs=[VMEM] * 3,
        out_shape=[
            jax.ShapeDtypeStruct((tok, 512), BF16),
            jax.ShapeDtypeStruct((n,) + state, F32),
            jax.ShapeDtypeStruct(state, BF16),
        ],
        scratch_shapes=[pltpu.VMEM(state, F32)],
        compiler_params=params(),
        cost_estimate=cost(n * 2 * 4 * 256 * 256 * 128, 4 * MIB),
        name="keys_stage",
    )(kvq, seed)


def local_body(q_ref, v_ref, kf_ref, seed_ref, before_ref, qf_ref, s_ref, num_ref, den_ref):
    mask = mask_of(CHUNK)
    for head in range(2):
        cols = slice(128 * head, 128 * head + 128)
        wide = slice(256 * head, 256 * head + 256)
        qf = features(q_ref[:, cols], seed_ref[head]).astype(BF16)
        qf_ref[:, wide] = qf
        scores = jnp.where(mask, dot(qf, kf_ref[:, wide], NT), 0.0)
        s16 = scores.astype(BF16)
        s_ref[:, wide] = s16
        main = before_ref[0, head, :128, :].astype(BF16)
        row = before_ref[0, head, 128:129, :]
        num_ref[:, cols] = dot(s16, v_ref[:, cols], NN) + dot(qf, main, NT)
        den_ref[head] = jnp.sum(scores, -1, keepdims=True) + jnp.sum(
            qf.astype(F32) * row, -1, keepdims=True
        )


def local_stage(kvq, kf, seed, before):
    tok = kvq.shape[0]
    n = tok // CHUNK
    return pl.pallas_call(
        local_body,
        grid=(n,),
        in_specs=[
            pl.BlockSpec((CHUNK, 256), lambda i: (i, 2)),
            pl.BlockSpec((CHUNK, 256), lambda i: (i, 1)),
            pl.BlockSpec((CHUNK, 512), lambda i: (i, 0)),
            pl.BlockSpec((2, 128, 256), lambda i: (0, 0, 0)),
            pl.BlockSpec((1, 2, STATE_ROWS, 256), lambda i: (i, 0, 0, 0)),
        ],
        out_specs=[
            pl.BlockSpec((CHUNK, 512), lambda i: (i, 0)),
            pl.BlockSpec((CHUNK, 512), lambda i: (i, 0)),
            pl.BlockSpec((CHUNK, 256), lambda i: (i, 0)),
            pl.BlockSpec((2, CHUNK, 1), lambda i: (0, i, 0)),
        ],
        out_shape=[
            jax.ShapeDtypeStruct((tok, 512), BF16),
            jax.ShapeDtypeStruct((tok, 512), BF16),
            jax.ShapeDtypeStruct((tok, 256), F32),
            jax.ShapeDtypeStruct((2, tok, 1), F32),
        ],
        compiler_params=params(),
        cost_estimate=cost(n * 2 * 10 * 256 * 256 * 128, 6 * MIB),
        name="local_stage",
    )(kvq, kvq, kf, seed, before)


def ratio_body(qf_ref, num_ref, den_ref, g_ref, prefix_ref, gn_ref, gd_ref, total_ref, carry_ref):
    carry_ref[...] = jnp.zeros_like(carry_ref)

    def chunk(i, rows):
        for head in range(2):
            cols = slice(128 * head, 128 * head + 128)
            main = prefix_ref[head, :128, :].astype(BF16)
            row = prefix_ref[head, 128:129, :]
            qf = qf_ref[rows, 256 * head : 256 * head + 256]
            qf32 = qf.astype(F32)
            num = num_ref[rows, cols] + dot(qf, main, NT)
            den = den_ref[head, rows] + jnp.sum(qf32 * row, -1, keepdims=True)
            inverse = 1.0 / den
            g = g_ref[rows, cols].astype(F32)
            gn = (g * inverse).astype(BF16)
            gd = -jnp.sum(g * num, -1, keepdims=True) * inverse * inverse
            gn_ref[rows, cols] = gn
            gd_ref[head, rows] = gd
            carry_ref[head, :128, :] += dot(gn, qf, TN)
            carry_ref[head, 128:129, :] += jnp.sum(qf32 * gd, 0, keepdims=True)

    over_chunks(qf_ref.shape[0] // CHUNK, chunk)
    total_ref[...] = carry_ref[...].astype(BF16)


def ratio_stage(qf, num, den, g, prefix):
    tok = qf.shape[0]
    n = tok // CHUNK
    state = (2, STATE_ROWS, 256)
    return pl.pallas_call(
        ratio_body,
        in_specs=[VMEM] * 5,
        out_specs=[VMEM] * 3,
        out_shape=[
            jax.ShapeDtypeStruct((tok, 256), BF16),
            jax.ShapeDtypeStruct((2, tok, 1), F32),
            jax.ShapeDtypeStruct(state, BF16),
        ],
        scratch_shapes=[pltpu.VMEM(state, F32)],
        compiler_params=params(),
        cost_estimate=cost(n * 2 * 4 * 256 * 256 * 128, 4 * MIB),
        name="ratio_stage",
    )(qf, num, den, g, prefix)


def middle_body(
    q_ref, v_ref, kf_ref, qf_ref, s_ref, gn_ref, gd_ref, seed_ref, before_ref, prefix_ref,
    dq_ref, dqt_ref, dkf_ref, dv_ref, carry_ref,
):
    step = pl.program_id(0)
    mask = mask_of(CHUNK)

    @pl.when(step == 0)
    def _():
        carry_ref[...] = jnp.zeros_like(carry_ref)

    for head in range(2):
        cols = slice(128 * head, 128 * head + 128)
        wide = slice(256 * head, 256 * head + 256)
        qf, kf, gn, gd = qf_ref[:, wide], kf_ref[:, wide], gn_ref[:, cols], gd_ref[head]
        v = v_ref[:, cols]
        qf32 = qf.astype(F32)
        pairs = jnp.where(mask, dot(gn, v, NT) + gd, 0.0).astype(BF16)
        earlier = prefix_ref[head] + before_ref[0, head]
        main, row = earlier[:128].astype(BF16), earlier[128:129]
        dqf = dot(pairs, kf, NN) + dot(gn, main, NN) + gd * row
        dq = feature_grad(dqf * qf32, q_ref[:, cols], seed_ref[head]).astype(BF16)
        dq_ref[:, cols] = dq
        dqt_ref[cols, :] = dq.T
        later = carry_ref[head]
        later_main, later_row = later[:128].astype(BF16), later[128:129]
        dkf_ref[:, wide] = dot(pairs, qf, TN) + dot(v, later_main, NN) + later_row
        dv_ref[:, cols] = dot(s_ref[:, wide], gn, TN) + dot(kf, later_main, NT)
        carry_ref[head, :128, :] += dot(gn, qf, TN)
        carry_ref[head, 128:129, :] += jnp.sum(qf32 * gd, 0, keepdims=True)


def middle_stage(kvq, kf, qf, s, gn, gd, seed, before, prefix):
    tok = qf.shape[0]
    n = tok // CHUNK
    state = (2, STATE_ROWS, 256)

    def narrow(column):
        return pl.BlockSpec((CHUNK, 256), lambda i: (n - 1 - i, column))

    wide = pl.BlockSpec((CHUNK, 512), lambda i: (n - 1 - i, 0))
    return pl.pallas_call(
        middle_body,
        grid=(n,),
        in_specs=[
            narrow(2), narrow(1), wide, wide, wide, narrow(0),
            pl.BlockSpec((2, CHUNK, 1), lambda i: (0, n - 1 - i, 0)),
            pl.BlockSpec((2, 128, 256), lambda i: (0, 0, 0)),
            pl.BlockSpec((1,) + state, lambda i: (n - 1 - i, 0, 0, 0)),
            pl.BlockSpec(state, lambda i: (0, 0, 0)),
        ],
        out_specs=[
            narrow(0),
            pl.BlockSpec((256, CHUNK), lambda i: (0, n - 1 - i)),
            wide,
            narrow(0),
        ],
        out_shape=[
            jax.ShapeDtypeStruct((tok, 256), BF16),
            jax.ShapeDtypeStruct((256, tok), BF16),
            jax.ShapeDtypeStruct((tok, 512), F32),
            jax.ShapeDtypeStruct((tok, 256), F32),
        ],
        scratch_shapes=[pltpu.VMEM(state, F32)],
        compiler_params=params(),
        cost_estimate=cost(n * 2 * 20 * 256 * 256 * 128, 10 * MIB),
        name="middle_stage",
    )(kvq, kvq, kf, qf, s, gn, gd, seed, before, prefix)


def last_body(kvq_ref, kf_ref, dkf_ref, dv_ref, seed_ref, suffix_ref, out_ref, outt_ref):
    def chunk(i, rows):
        for head in range(2):
            cols = slice(128 * head, 128 * head + 128)
            wide = slice(256 * head, 256 * head + 256)
            dv_cols = slice(256 + 128 * head, 384 + 128 * head)
            main = suffix_ref[head, :128, :].astype(BF16)
            row = suffix_ref[head, 128:129, :]
            kf = kf_ref[rows, wide]
            dkf = dkf_ref[rows, wide] + dot(kvq_ref[rows, dv_cols], main, NN) + row
            dk = feature_grad(dkf * kf.astype(F32), kvq_ref[rows, cols], seed_ref[head])
            dk = dk.astype(BF16)
            dv = (dv_ref[rows, cols] + dot(kf, main, NT)).astype(BF16)
            out_ref[rows, cols] = dk
            out_ref[rows, dv_cols] = dv
            outt_ref[cols, rows] = dk.T
            outt_ref[dv_cols, rows] = dv.T

    over_chunks(kvq_ref.shape[0] // CHUNK, chunk)


def last_stage(kvq, kf, dkf, dv, seed, suffix):
    tok = kf.shape[0]
    n = tok // CHUNK
    return pl.pallas_call(
        last_body,
        in_specs=[VMEM] * 6,
        out_specs=[VMEM] * 2,
        out_shape=[
            jax.ShapeDtypeStruct((tok, 512), BF16),
            jax.ShapeDtypeStruct((512, tok), BF16),
        ],
        compiler_params=params(),
        cost_estimate=cost(n * 2 * 6 * 256 * 256 * 128, 6 * MIB),
        name="last_stage",
    )(kvq, kf, dkf, dv, seed, suffix)


def early_body(x_ref, d_ref, out_ref):
    out_ref[...] = dot(x_ref[...], d_ref[...], NN)


def wgrad_body(x_ref, dkv_ref, early_ref, out_ref):
    out_ref[:, :512] = dot(x_ref[...], dkv_ref[...], NN)
    out_ref[:, 512:] = early_ref[...]


def wgrad_call(body, x, d, early, columns):
    depth, tok = x.shape
    size = 256
    specs = [pl.BlockSpec((size, tok), lambda i: (i, 0)), pl.BlockSpec(d.shape, lambda i: (0, 0))]
    specs += [pl.BlockSpec((size, a.shape[1]), lambda i: (i, 0)) for a in early]

    return pl.pallas_call(
        body,
        grid=(depth // size,),
        in_specs=specs,
        out_specs=pl.BlockSpec((size, columns), lambda i: (i, 0)),
        out_shape=jax.ShapeDtypeStruct((depth, columns), F32),
        compiler_params=params(),
        cost_estimate=cost(2 * tok * depth * columns, 6 * MIB),
    )(x, d, *early)


def finish_body(core_ref, keep_ref, got_ref, q_ref, k_ref, v_ref):
    core = core_ref[0]
    mine = pl.ds(pl.multiple_of(core * 256, 256), 256)
    theirs = pl.ds(pl.multiple_of((1 - core) * 256, 256), 256)
    for place, ref in enumerate((k_ref, v_ref, q_ref)):
        cols = slice(256 * place, 256 * place + 256)
        ref[:, mine] = keep_ref[:, cols].astype(F32)
        ref[:, theirs] = got_ref[:, cols].astype(F32)


def finish(core, keep, got):
    rows = keep.shape[0]
    out = jax.ShapeDtypeStruct((rows, 512), F32)
    whole = pl.BlockSpec(keep.shape, lambda i, core: (0, 0))
    return pl.pallas_call(
        finish_body,
        out_shape=[out] * 3,
        grid_spec=pltpu.PrefetchScalarGridSpec(
            num_scalar_prefetch=1,
            grid=(1,),
            in_specs=[whole, whole],
            out_specs=[pl.BlockSpec((rows, 512), lambda i, core: (0, 0))] * 3,
        ),
        compiler_params=params(8),
        cost_estimate=cost(MIB, MIB),
        name="finish",
    )(core, keep, got)


def collect_body(place_ref, *refs):
    *pieces, out_ref, sems = refs
    size = pieces[0].shape[0] // 2
    copies = []
    for slot in range(2 * len(pieces)):
        to = pl.ds(pl.multiple_of(place_ref[slot] * size, size), size)
        source = pieces[slot // 2].at[pl.ds(slot % 2 * size, size), :]
        copies.append(pltpu.make_async_copy(source, out_ref.at[to, :], sems.at[slot]))
    for copy in copies:
        copy.start()
    for copy in copies:
        copy.wait()


def collect(place, pieces):
    rows, columns = pieces[0].shape
    n = len(pieces)
    return pl.pallas_call(
        collect_body,
        out_shape=jax.ShapeDtypeStruct((n * rows, columns), BF16),
        grid_spec=pltpu.PrefetchScalarGridSpec(
            num_scalar_prefetch=1,
            grid=(1,),
            in_specs=[pl.BlockSpec((rows, columns), lambda i, place: (0, 0))] * n,
            out_specs=pl.BlockSpec(memory_space=pl.ANY),
            scratch_shapes=[pltpu.SemaphoreType.DMA((2 * n,))],
        ),
        compiler_params=params(16),
        cost_estimate=cost(MIB, 12 * MIB),
        name="collect",
    )(place, *pieces)


def back_body(place_ref, mkv_ref, mq_ref, tkv_ref, tq_ref, wm_ref, wt_ref, out_ref):
    out_ref[...] = (
        dot(wm_ref[:, :512], mkv_ref[...], NN)
        + dot(wm_ref[:, 512:], mq_ref[...], NN)
        + dot(wt_ref[:, :512], tkv_ref[...], NN)
        + dot(wt_ref[:, 512:], tq_ref[...], NN)
    )


def back(place, dkvt, dqt, theirs_kv, theirs_q, w_mine, w_theirs):
    rows = theirs_kv.shape[1]
    depth = w_mine.shape[1]
    width = 512
    n = place.shape[0] - 1

    def half_of(a):
        return pl.BlockSpec((a.shape[0], rows), lambda k, p: (0, p[0]))

    def whole(a):
        return pl.BlockSpec(a.shape, lambda k, p: (0, 0))

    weights = pl.BlockSpec((width, depth), lambda k, p: (p[1 + k], 0))
    return pl.pallas_call(
        back_body,
        out_shape=jax.ShapeDtypeStruct((n * width, rows), F32),
        grid_spec=pltpu.PrefetchScalarGridSpec(
            num_scalar_prefetch=1,
            grid=(n,),
            in_specs=[
                half_of(dkvt), half_of(dqt), whole(theirs_kv), whole(theirs_q), weights, weights,
            ],
            out_specs=pl.BlockSpec((width, rows), lambda k, p: (k, 0)),
        ),
        compiler_params=params(),
        cost_estimate=cost(4 * rows * n * width * depth, 8 * MIB),
        name="back",
    )(place, dkvt, dqt, theirs_kv, theirs_q, w_mine, w_theirs)


def turn_body(own_ref, at_ref, ab_ref, bt_ref, bb_ref, out_ref):
    upper = pl.program_id(0) < pl.num_programs(0) // 2
    after = jnp.where(upper, at_ref[...].astype(F32), ab_ref[...].astype(F32))
    before = jnp.where(upper, bt_ref[...].astype(F32), bb_ref[...].astype(F32))
    out_ref[...] = (own_ref[...] + after + before).astype(BF16).T


def turn(own, after, before):
    columns, rows = own.shape
    size = 256
    n = columns // size
    part = pl.BlockSpec((size, rows), lambda i: (i, 0))
    top = pl.BlockSpec((size, rows), lambda i: (jnp.minimum(i, n // 2 - 1), 0))
    bottom = pl.BlockSpec((size, rows), lambda i: (jnp.maximum(i - n // 2, 0), 0))
    return pl.pallas_call(
        turn_body,
        grid=(n,),
        in_specs=[part, top, bottom, top, bottom],
        out_specs=pl.BlockSpec((rows, size), lambda i: (0, i)),
        out_shape=jax.ShapeDtypeStruct((rows, columns), BF16),
        compiler_params=params(),
        cost_estimate=cost(4 * MIB, 6 * MIB),
        name="turn",
    )(own, *after, *before)


def swap(a):
    return lax.ppermute(a, "c", SWAP)


def ring(a, axis, by):
    return lax.ppermute(a, axis, [(i, (i + by) % 4) for i in range(4)])


def along(a, by, inner):
    pairs = []
    for z in range(4):
        for y in range(4):
            for c in range(2):
                over_y = (c == 0) == inner
                to = (z, (y + by) % 4) if over_y else ((z + by) % 4, y)
                pairs.append(((z * 4 + y) * 2 + c, (to[0] * 4 + to[1]) * 2 + c))
    return lax.ppermute(a, ("z", "y", "c"), pairs)


def gather_ring(a):
    half = a.shape[0] // 2
    before = along(a, 1, True)
    after = along(a, -1, True)
    top = along(before[:half], 1, True)
    bottom = along(after[half:], -1, True)
    return a, after, top, bottom, before


def gather_halves(top, bottom):
    top3 = along(top, 1, False)
    bottom1 = along(bottom, -1, False)
    bottom3 = along(bottom, 1, False)
    top1 = along(top, -1, False)
    top2 = along(top3, 1, False)
    bottom2 = along(bottom1, -1, False)
    return (top, bottom), (top1, bottom1), (top2, bottom2), (top3, bottom3)


def scatter_ring(far, after, before, send):
    far = far.astype(BF16)
    half = far.shape[0] // 2
    top = send(far[:half], 1).astype(F32)
    bottom = send(far[half:], -1).astype(F32)
    after_plain = send(after[half:].astype(BF16), 1)
    before_plain = send(before[:half].astype(BF16), -1)
    after_sum = send((after[:half] + top).astype(BF16), 1)
    before_sum = send((before[half:] + bottom).astype(BF16), -1)
    return (after_sum, after_plain), (before_plain, before_sum)


def scatter_small(part):
    far = part(2).astype(BF16)
    half = far.shape[0] // 2
    top = along(far[:half], 1, True).astype(F32)
    bottom = along(far[half:], -1, True).astype(F32)
    after, before = part(1), part(3)
    after = jnp.concatenate([after[:half] + top, after[half:]], 0).astype(BF16)
    before = jnp.concatenate([before[:half], before[half:] + bottom], 0).astype(BF16)
    after = along(after, 1, True).astype(F32)
    before = along(before, -1, True).astype(F32)
    return part(0) + after + before


def scan_flags(inner, outer, direction):
    inner = inner if direction == 1 else 3 - inner
    outer = outer if direction == 1 else 3 - outer
    return tuple((inner >= by, outer + by > 3) for by in (1, 3, 2))


def scan_chips(state, first, flags, direction):
    near = [along(state, direction * by, True).astype(F32) for by in (1, 3, 2)]
    own = state.astype(F32)
    ahead = jnp.zeros_like(own)
    for (passed, _), a in zip(flags, near):
        ahead = ahead + jnp.where(passed, a, 0.0)
    every = near[0] + near[1] + near[2] + own
    straight = jnp.where(first, every, ahead + own).astype(BF16)
    wrapped = jnp.where(first, 0.0, ahead).astype(BF16)
    total = ahead
    for by, (_, wraps) in zip((1, 3, 2), flags):
        message = jnp.where(wraps, wrapped, straight)
        total = total + along(message, direction * by, False).astype(F32)
    return total


def in_order(first, mine, theirs, axis=0):
    one = jnp.where(first, mine, theirs)
    two = jnp.where(first, theirs, mine)
    return jnp.concatenate([one, two], axis)


def half_of(first, a, axis):
    size = a.shape[axis] // 2
    low = lax.slice_in_dim(a, 0, size, axis=axis)
    high = lax.slice_in_dim(a, size, 2 * size, axis=axis)
    return jnp.where(first, low, high), jnp.where(first, high, low)


def per_device(tokens, w_query, w_key, w_value, omega_seed, grad_out):
    core, x, y, z = (lax.axis_index(name).astype(jnp.int32) for name in ("c", "x", "y", "z"))
    outer, inner = jnp.where(core == 0, z, y), jnp.where(core == 0, y, z)
    step = jnp.arange(4, dtype=jnp.int32)
    along_outer, along_inner = (outer + step) % 4, (inner + step) % 4
    chip = jnp.where(
        core == 0,
        along_outer[:, None] * 4 + along_inner[None, :],
        along_inner[None, :] * 4 + along_outer[:, None],
    ).reshape(16)

    def place_of(*steps):
        rows = [2 * lax.rem(x + by, 4) + i for by in steps for i in range(2)]
        return jnp.stack([core] + rows)

    where = (
        core == 0,
        jnp.concatenate([chip, core[None]]),
        chip,
        core[None],
        place_of(2),
        place_of(1, 3),
        place_of(0),
        scan_flags(inner, outer, 1),
        scan_flags(inner, outer, -1),
    )
    where, tokens, w_query, w_key, w_value, omega_seed, grad_out = lax.optimization_barrier(
        (where, tokens, w_query, w_key, w_value, omega_seed, grad_out)
    )
    first, idx, chip, core, far_place, side_place, own_place, ahead_flags, behind_flags = where

    w_mine, w_give = halve(core, (w_key, w_value, w_query))
    w_chip = in_order(first, w_mine, swap(w_give))
    g_got = swap(grad_out)
    g = in_order(first, half_of(first, grad_out, 1)[0], half_of(first, g_got, 1)[0])
    other = swap(tokens)
    seed = half_of(first, omega_seed, 0)[0].astype(BF16)

    w0, w1, w2_top, w2_bottom, w3 = gather_ring(w_chip)
    w_groups = gather_halves(
        jnp.concatenate([w0, w1], 0), jnp.concatenate([w2_top, w2_bottom, w3], 0)
    )
    arranged = [arrange(idx, tokens, other, a) for a in range(4)]
    xs = [a[0] for a in arranged]
    acc = project(first_body, [], [xs[0]], list(w_groups[0]), F32)
    pieces = list(w_groups[1] + w_groups[3])
    acc = project(more_body, [acc], [xs[1], xs[3]], pieces, F32)
    top, bottom = w_groups[2]
    acc = project(top_body, [acc], [xs[2]], [top], F32)
    kvq = project(end_body, [acc], [xs[2]], [bottom], BF16)

    kf, before, total = keys_stage(kvq, seed)
    prefix = scan_chips(total, first, ahead_flags, 1)
    weights = collect(chip, [p for pair in w_groups for p in pair])
    weights_theirs = swap(weights)
    qf, s, num, den = local_stage(kvq, kf, seed, before)
    gn, gd, later = ratio_stage(qf, num, den, g, prefix)
    suffix = scan_chips(later, first, behind_flags, -1)
    dq, dqt, dkf, dv = middle_stage(kvq, kf, qf, s, gn, gd, seed, before, prefix)
    dkv, dkvt = last_stage(kvq, kf, dkf, dv, seed, suffix)

    theirs_q = swap(half_of(first, dqt, 1)[1])
    theirs_kv = swap(half_of(first, dkvt, 1)[1])

    def group(a):
        x_rows = arranged[a][1]
        early = wgrad_call(early_body, x_rows, dq, [], 256)
        return wgrad_call(wgrad_body, x_rows, dkv, [early], 768)

    def quarters(place):
        return back(place, dkvt, dqt, theirs_kv, theirs_q, weights, weights_theirs)

    after, before = scatter_ring(group(2), group(1), group(3), lambda a, by: along(a, by, False))
    own = group(0)
    half = own.shape[0] // 2
    row_sum = [
        own[i * half : (i + 1) * half] + after[i].astype(F32) + before[i].astype(F32)
        for i in range(2)
    ]

    def strip_of(b):
        size = half // 2
        return row_sum[b // 2][b % 2 * size : (b % 2 + 1) * size]

    total_w = scatter_small(strip_of).astype(BF16)

    sides = quarters(side_place)
    columns = sides.shape[0] // 2
    after, before = scatter_ring(
        quarters(far_place), sides[:columns], sides[columns:], lambda a, by: ring(a, "x", by)
    )
    input_grad = turn(quarters(own_place), after, before)

    keep, give = half_of(first, total_w, 0)
    return input_grad, *finish(core, keep, swap(give))


def solution(mesh):
    chips = Mesh(mesh.devices.reshape(4, 4, 2, 4), ("z", "y", "c", "x"))
    seq = ("z", "y", "c")
    placed = (
        P(seq, None),
        P(seq, "x"),
        P(seq, "x"),
        P(seq, "x"),
        P("x", None, None),
        P(seq, "x"),
    )
    specs = (P(seq, "x"), P(seq, "x"), P(seq, "x"), P(seq, "x"))

    return jax.shard_map(per_device, mesh=chips, in_specs=placed, out_specs=specs, check_vma=False)
```

```python
import math

import jax
import jax.numpy as jnp
from jax import lax
from jax.experimental import pallas as pl
from jax.experimental.pallas import tpu as pltpu
from jax.sharding import Mesh, PartitionSpec as P


F32 = jnp.float32
BF16 = jnp.bfloat16
SEED_STEP = 0.4
CHUNK = 256
NT = (((1,), (1,)), ((), ()))
TN = (((0,), (0,)), ((), ()))
NN = (((1,), (0,)), ((), ()))
SWAP = ((0, 1), (1, 0))
STATE_ROWS = 144
MIB = 1 << 20


def dot(a, b, dims):
    return lax.dot_general(a, b, dims, preferred_element_type=F32)


GRANT = 12


VMEM = pl.BlockSpec(memory_space=pltpu.VMEM)
SMEM = pl.BlockSpec(memory_space=pltpu.SMEM)


def over_rows(count, size, body):
    def step(i, _):
        body(i, pl.ds(pl.multiple_of(i * size, size), size))

    lax.fori_loop(0, count // size, step, None)


def params(vmem=GRANT):
    return pltpu.CompilerParams(vmem_limit_bytes=vmem * MIB)


def cost(flops, nbytes):
    return pl.CostEstimate(flops=flops, bytes_accessed=nbytes, transcendentals=0)


def halve_body(core_ref, *refs):
    *sources, mine_ref, give_ref = refs
    core = core_ref[0]
    half = sources[0].shape[1] // 2
    mine = pl.ds(pl.multiple_of(core * half, half), half)
    give = pl.ds(pl.multiple_of((1 - core) * half, half), half)
    for i, ref in enumerate(sources):
        cols = slice(half * i, half * i + half)
        mine_ref[:, cols] = ref[:, mine]
        give_ref[:, cols] = ref[:, give]


def halve(core, sources):
    size, columns = sources[0].shape
    whole = pl.BlockSpec((size, columns), lambda i, core: (0, 0))
    shape = (size, len(sources) * columns // 2)
    return pl.pallas_call(
        halve_body,
        out_shape=[jax.ShapeDtypeStruct(shape, BF16)] * 2,
        grid_spec=pltpu.PrefetchScalarGridSpec(
            num_scalar_prefetch=1,
            grid=(1,),
            in_specs=[whole] * len(sources),
            out_specs=[pl.BlockSpec(shape, lambda i, core: (0, 0))] * 2,
        ),
        compiler_params=params(56),
        cost_estimate=cost(MIB, MIB),
        name="halve",
    )(core, *sources)


def arrange_body(idx_ref, own_ref, other_ref, rows_ref, columns_ref):
    core = idx_ref[16]
    size = own_ref.shape[0]
    mine = pl.ds(pl.multiple_of(core * size, size), size)
    theirs = pl.ds(pl.multiple_of((1 - core) * size, size), size)
    own, other = own_ref[...], other_ref[...]
    rows_ref[mine, :] = own
    rows_ref[theirs, :] = other
    columns_ref[:, mine] = own.T
    columns_ref[:, theirs] = other.T


def arrange(idx, own, other, group):
    size, depth = own.shape
    width = depth // 16
    source = pl.BlockSpec((size, width), lambda k, idx: (0, idx[4 * group + k]))
    return pl.pallas_call(
        arrange_body,
        out_shape=[
            jax.ShapeDtypeStruct((2 * size, 4 * width), BF16),
            jax.ShapeDtypeStruct((4 * width, 2 * size), BF16),
        ],
        grid_spec=pltpu.PrefetchScalarGridSpec(
            num_scalar_prefetch=1,
            grid=(4,),
            in_specs=[source, source],
            out_specs=[
                pl.BlockSpec((2 * size, width), lambda k, idx: (0, k)),
                pl.BlockSpec((width, 2 * size), lambda k, idx: (k, 0)),
            ],
        ),
        compiler_params=params(),
        cost_estimate=cost(4 * MIB, 6 * MIB),
        name="arrange",
    )(idx, own, other)


def halves_dot(x_ref, rows, wa_ref, wb_ref):
    half = wa_ref.shape[0]
    return dot(x_ref[rows, :half], wa_ref[...], NN) + dot(x_ref[rows, half:], wb_ref[...], NN)


def first_body(x_ref, wa_ref, wb_ref, out_ref):
    def block(_, rows):
        out_ref[rows, :] = halves_dot(x_ref, rows, wa_ref, wb_ref)

    over_rows(out_ref.shape[0], CHUNK, block)


def more_body(acc_ref, xa_ref, xb_ref, *rest):
    *w_refs, out_ref = rest

    def block(_, rows):
        total = acc_ref[rows, :]
        for x_ref, pair in ((xa_ref, w_refs[:2]), (xb_ref, w_refs[2:])):
            total += halves_dot(x_ref, rows, *pair)
        out_ref[rows, :] = total

    over_rows(out_ref.shape[0], CHUNK, block)


def top_body(acc_ref, x_ref, w_ref, out_ref):
    def block(_, rows):
        out_ref[rows, :] = acc_ref[rows, :] + dot(x_ref[rows, : w_ref.shape[0]], w_ref[...], NN)

    over_rows(out_ref.shape[0], CHUNK, block)


def end_body(acc_ref, x_ref, w_ref, out_ref):
    def block(_, rows):
        out = acc_ref[rows, :] + dot(x_ref[rows, w_ref.shape[0] :], w_ref[...], NN)
        out_ref[rows, :] = out.astype(BF16)

    over_rows(out_ref.shape[0], CHUNK, block)


def project(body, acc, xs, ws, dtype):
    tok = xs[0].shape[0]
    columns = ws[0].shape[1]
    ops = acc + xs + ws
    depth = sum(w.shape[0] for w in ws)
    return pl.pallas_call(
        body,
        in_specs=[VMEM] * len(ops),
        out_specs=VMEM,
        out_shape=jax.ShapeDtypeStruct((tok, columns), dtype),
        compiler_params=params(),
        cost_estimate=cost(2 * tok * depth * columns, 8 * MIB),
    )(*ops)


def features(rows, seed):
    size = rows.shape[1]
    scale = size ** (-0.25)
    scaled = rows.astype(F32) * scale
    projected = dot(rows, seed, NN) * (SEED_STEP * scale)
    norm = 0.5 * jnp.sum(scaled * scaled, -1, keepdims=True)
    return jnp.exp(projected - norm) * (1.0 / math.sqrt(seed.shape[1]))


def feature_grad(weighted, rows, seed):
    scale = rows.shape[1] ** (-0.25)
    projected = dot(weighted.astype(BF16), seed, NT) * SEED_STEP
    total = jnp.sum(weighted, -1, keepdims=True)
    return (projected - total * (rows.astype(F32) * scale)) * scale


def mask_of(size):
    return lax.broadcasted_iota(jnp.int32, (size, size), 0) >= lax.broadcasted_iota(
        jnp.int32, (size, size), 1
    )


PER_STEP = 2


def over_chunks(n, body):
    def step(i, _):
        for part in range(PER_STEP):
            start = (i * PER_STEP + part) * CHUNK
            body(i * PER_STEP + part, pl.ds(pl.multiple_of(start, CHUNK), CHUNK))

    lax.fori_loop(0, n // PER_STEP, step, None)


def keys_body(kvq_ref, seed_ref, kf_ref, before_ref, total_ref, carry_ref):
    carry_ref[...] = jnp.zeros_like(carry_ref)
    pad = jnp.zeros((STATE_ROWS - 129, 256), F32)

    def chunk(i, rows):
        for head in range(2):
            state = carry_ref[head]
            before_ref[i, head] = state
            kf = features(kvq_ref[rows, 128 * head : 128 * head + 128], seed_ref[head])
            kf = kf.astype(BF16)
            kf_ref[rows, 256 * head : 256 * head + 256] = kf
            main = dot(kvq_ref[rows, 256 + 128 * head : 384 + 128 * head], kf, TN)
            row = jnp.sum(kf.astype(F32), 0, keepdims=True)
            carry_ref[head] = state + jnp.concatenate([main, row, pad], 0)

    over_chunks(kvq_ref.shape[0] // CHUNK, chunk)
    total_ref[...] = carry_ref[...].astype(BF16)


def keys_stage(kvq, seed):
    tok = kvq.shape[0]
    n = tok // CHUNK
    state = (2, STATE_ROWS, 256)
    return pl.pallas_call(
        keys_body,
        in_specs=[VMEM] * 2,
        out_specs=[VMEM] * 3,
        out_shape=[
            jax.ShapeDtypeStruct((tok, 512), BF16),
            jax.ShapeDtypeStruct((n,) + state, F32),
            jax.ShapeDtypeStruct(state, BF16),
        ],
        scratch_shapes=[pltpu.VMEM(state, F32)],
        compiler_params=params(),
        cost_estimate=cost(n * 2 * 4 * 256 * 256 * 128, 4 * MIB),
        name="keys_stage",
    )(kvq, seed)


def local_body(q_ref, v_ref, kf_ref, seed_ref, before_ref, qf_ref, s_ref, num_ref, den_ref):
    mask = mask_of(CHUNK)
    for head in range(2):
        cols = slice(128 * head, 128 * head + 128)
        wide = slice(256 * head, 256 * head + 256)
        qf = features(q_ref[:, cols], seed_ref[head]).astype(BF16)
        qf_ref[:, wide] = qf
        scores = jnp.where(mask, dot(qf, kf_ref[:, wide], NT), 0.0)
        s16 = scores.astype(BF16)
        s_ref[:, wide] = s16
        main = before_ref[0, head, :128, :].astype(BF16)
        row = before_ref[0, head, 128:129, :]
        num_ref[:, cols] = dot(s16, v_ref[:, cols], NN) + dot(qf, main, NT)
        den_ref[head] = jnp.sum(scores, -1, keepdims=True) + jnp.sum(
            qf.astype(F32) * row, -1, keepdims=True
        )


def local_stage(kvq, kf, seed, before):
    tok = kvq.shape[0]
    n = tok // CHUNK
    return pl.pallas_call(
        local_body,
        grid=(n,),
        in_specs=[
            pl.BlockSpec((CHUNK, 256), lambda i: (i, 2)),
            pl.BlockSpec((CHUNK, 256), lambda i: (i, 1)),
            pl.BlockSpec((CHUNK, 512), lambda i: (i, 0)),
            pl.BlockSpec((2, 128, 256), lambda i: (0, 0, 0)),
            pl.BlockSpec((1, 2, STATE_ROWS, 256), lambda i: (i, 0, 0, 0)),
        ],
        out_specs=[
            pl.BlockSpec((CHUNK, 512), lambda i: (i, 0)),
            pl.BlockSpec((CHUNK, 512), lambda i: (i, 0)),
            pl.BlockSpec((CHUNK, 256), lambda i: (i, 0)),
            pl.BlockSpec((2, CHUNK, 1), lambda i: (0, i, 0)),
        ],
        out_shape=[
            jax.ShapeDtypeStruct((tok, 512), BF16),
            jax.ShapeDtypeStruct((tok, 512), BF16),
            jax.ShapeDtypeStruct((tok, 256), F32),
            jax.ShapeDtypeStruct((2, tok, 1), F32),
        ],
        compiler_params=params(),
        cost_estimate=cost(n * 2 * 10 * 256 * 256 * 128, 6 * MIB),
        name="local_stage",
    )(kvq, kvq, kf, seed, before)


def ratio_body(qf_ref, num_ref, den_ref, g_ref, prefix_ref, gn_ref, gd_ref, total_ref, carry_ref):
    carry_ref[...] = jnp.zeros_like(carry_ref)

    def chunk(i, rows):
        for head in range(2):
            cols = slice(128 * head, 128 * head + 128)
            main = prefix_ref[head, :128, :].astype(BF16)
            row = prefix_ref[head, 128:129, :]
            qf = qf_ref[rows, 256 * head : 256 * head + 256]
            qf32 = qf.astype(F32)
            num = num_ref[rows, cols] + dot(qf, main, NT)
            den = den_ref[head, rows] + jnp.sum(qf32 * row, -1, keepdims=True)
            inverse = 1.0 / den
            g = g_ref[rows, cols].astype(F32)
            gn = (g * inverse).astype(BF16)
            gd = -jnp.sum(g * num, -1, keepdims=True) * inverse * inverse
            gn_ref[rows, cols] = gn
            gd_ref[head, rows] = gd
            carry_ref[head, :128, :] += dot(gn, qf, TN)
            carry_ref[head, 128:129, :] += jnp.sum(qf32 * gd, 0, keepdims=True)

    over_chunks(qf_ref.shape[0] // CHUNK, chunk)
    total_ref[...] = carry_ref[...].astype(BF16)


def ratio_stage(qf, num, den, g, prefix):
    tok = qf.shape[0]
    n = tok // CHUNK
    state = (2, STATE_ROWS, 256)
    return pl.pallas_call(
        ratio_body,
        in_specs=[VMEM] * 5,
        out_specs=[VMEM] * 3,
        out_shape=[
            jax.ShapeDtypeStruct((tok, 256), BF16),
            jax.ShapeDtypeStruct((2, tok, 1), F32),
            jax.ShapeDtypeStruct(state, BF16),
        ],
        scratch_shapes=[pltpu.VMEM(state, F32)],
        compiler_params=params(),
        cost_estimate=cost(n * 2 * 4 * 256 * 256 * 128, 4 * MIB),
        name="ratio_stage",
    )(qf, num, den, g, prefix)


def middle_body(
    q_ref, v_ref, kf_ref, qf_ref, s_ref, gn_ref, gd_ref, seed_ref, before_ref, prefix_ref,
    dq_ref, dqt_ref, dkf_ref, dv_ref, carry_ref,
):
    step = pl.program_id(0)
    mask = mask_of(CHUNK)

    @pl.when(step == 0)
    def _():
        carry_ref[...] = jnp.zeros_like(carry_ref)

    for head in range(2):
        cols = slice(128 * head, 128 * head + 128)
        wide = slice(256 * head, 256 * head + 256)
        qf, kf, gn, gd = qf_ref[:, wide], kf_ref[:, wide], gn_ref[:, cols], gd_ref[head]
        v = v_ref[:, cols]
        qf32 = qf.astype(F32)
        pairs = jnp.where(mask, dot(gn, v, NT) + gd, 0.0).astype(BF16)
        earlier = prefix_ref[head] + before_ref[0, head]
        main, row = earlier[:128].astype(BF16), earlier[128:129]
        dqf = dot(pairs, kf, NN) + dot(gn, main, NN) + gd * row
        dq = feature_grad(dqf * qf32, q_ref[:, cols], seed_ref[head]).astype(BF16)
        dq_ref[:, cols] = dq
        dqt_ref[cols, :] = dq.T
        later = carry_ref[head]
        later_main, later_row = later[:128].astype(BF16), later[128:129]
        dkf_ref[:, wide] = dot(pairs, qf, TN) + dot(v, later_main, NN) + later_row
        dv_ref[:, cols] = dot(s_ref[:, wide], gn, TN) + dot(kf, later_main, NT)
        carry_ref[head, :128, :] += dot(gn, qf, TN)
        carry_ref[head, 128:129, :] += jnp.sum(qf32 * gd, 0, keepdims=True)


def middle_stage(kvq, kf, qf, s, gn, gd, seed, before, prefix):
    tok = qf.shape[0]
    n = tok // CHUNK
    state = (2, STATE_ROWS, 256)

    def narrow(column):
        return pl.BlockSpec((CHUNK, 256), lambda i: (n - 1 - i, column))

    wide = pl.BlockSpec((CHUNK, 512), lambda i: (n - 1 - i, 0))
    return pl.pallas_call(
        middle_body,
        grid=(n,),
        in_specs=[
            narrow(2), narrow(1), wide, wide, wide, narrow(0),
            pl.BlockSpec((2, CHUNK, 1), lambda i: (0, n - 1 - i, 0)),
            pl.BlockSpec((2, 128, 256), lambda i: (0, 0, 0)),
            pl.BlockSpec((1,) + state, lambda i: (n - 1 - i, 0, 0, 0)),
            pl.BlockSpec(state, lambda i: (0, 0, 0)),
        ],
        out_specs=[
            narrow(0),
            pl.BlockSpec((256, CHUNK), lambda i: (0, n - 1 - i)),
            wide,
            narrow(0),
        ],
        out_shape=[
            jax.ShapeDtypeStruct((tok, 256), BF16),
            jax.ShapeDtypeStruct((256, tok), BF16),
            jax.ShapeDtypeStruct((tok, 512), F32),
            jax.ShapeDtypeStruct((tok, 256), F32),
        ],
        scratch_shapes=[pltpu.VMEM(state, F32)],
        compiler_params=params(),
        cost_estimate=cost(n * 2 * 20 * 256 * 256 * 128, 10 * MIB),
        name="middle_stage",
    )(kvq, kvq, kf, qf, s, gn, gd, seed, before, prefix)


def last_body(kvq_ref, kf_ref, dkf_ref, dv_ref, seed_ref, suffix_ref, out_ref, outt_ref):
    def chunk(i, rows):
        for head in range(2):
            cols = slice(128 * head, 128 * head + 128)
            wide = slice(256 * head, 256 * head + 256)
            dv_cols = slice(256 + 128 * head, 384 + 128 * head)
            main = suffix_ref[head, :128, :].astype(BF16)
            row = suffix_ref[head, 128:129, :]
            kf = kf_ref[rows, wide]
            dkf = dkf_ref[rows, wide] + dot(kvq_ref[rows, dv_cols], main, NN) + row
            dk = feature_grad(dkf * kf.astype(F32), kvq_ref[rows, cols], seed_ref[head])
            dk = dk.astype(BF16)
            dv = (dv_ref[rows, cols] + dot(kf, main, NT)).astype(BF16)
            out_ref[rows, cols] = dk
            out_ref[rows, dv_cols] = dv
            outt_ref[cols, rows] = dk.T
            outt_ref[dv_cols, rows] = dv.T

    over_chunks(kvq_ref.shape[0] // CHUNK, chunk)


def last_stage(kvq, kf, dkf, dv, seed, suffix):
    tok = kf.shape[0]
    n = tok // CHUNK
    return pl.pallas_call(
        last_body,
        in_specs=[VMEM] * 6,
        out_specs=[VMEM] * 2,
        out_shape=[
            jax.ShapeDtypeStruct((tok, 512), BF16),
            jax.ShapeDtypeStruct((512, tok), BF16),
        ],
        compiler_params=params(),
        cost_estimate=cost(n * 2 * 6 * 256 * 256 * 128, 6 * MIB),
        name="last_stage",
    )(kvq, kf, dkf, dv, seed, suffix)


def early_body(x_ref, d_ref, out_ref):
    def block(_, rows):
        out_ref[rows, :] = dot(x_ref[rows, :], d_ref[...], NN)

    over_rows(out_ref.shape[0], 512, block)


def wgrad_body(x_ref, dkv_ref, early_ref, out_ref):
    def block(_, rows):
        out_ref[rows, :512] = dot(x_ref[rows, :], dkv_ref[...], NN)
        out_ref[rows, 512:] = early_ref[rows, :]

    over_rows(out_ref.shape[0], 512, block)


def wgrad_call(body, x, d, early, columns):
    depth, tok = x.shape
    return pl.pallas_call(
        body,
        in_specs=[VMEM] * (2 + len(early)),
        out_specs=VMEM,
        out_shape=jax.ShapeDtypeStruct((depth, columns), F32),
        compiler_params=params(),
        cost_estimate=cost(2 * tok * depth * columns, 6 * MIB),
    )(x, d, *early)


def finish_body(core_ref, keep_ref, got_ref, q_ref, k_ref, v_ref):
    core = core_ref[0]
    mine = pl.ds(pl.multiple_of(core * 256, 256), 256)
    theirs = pl.ds(pl.multiple_of((1 - core) * 256, 256), 256)
    for place, ref in enumerate((k_ref, v_ref, q_ref)):
        cols = slice(256 * place, 256 * place + 256)
        ref[:, mine] = keep_ref[:, cols].astype(F32)
        ref[:, theirs] = got_ref[:, cols].astype(F32)


def finish(core, keep, got):
    rows = keep.shape[0]
    out = jax.ShapeDtypeStruct((rows, 512), F32)
    whole = pl.BlockSpec(keep.shape, lambda i, core: (0, 0))
    return pl.pallas_call(
        finish_body,
        out_shape=[out] * 3,
        grid_spec=pltpu.PrefetchScalarGridSpec(
            num_scalar_prefetch=1,
            grid=(1,),
            in_specs=[whole, whole],
            out_specs=[pl.BlockSpec((rows, 512), lambda i, core: (0, 0))] * 3,
        ),
        compiler_params=params(8),
        cost_estimate=cost(MIB, MIB),
        name="finish",
    )(core, keep, got)


def collect_body(place_ref, *refs):
    *pieces, out_ref, sems = refs
    size = pieces[0].shape[0] // 2
    copies = []
    for slot in range(2 * len(pieces)):
        to = pl.ds(pl.multiple_of(place_ref[slot] * size, size), size)
        source = pieces[slot // 2].at[pl.ds(slot % 2 * size, size), :]
        copies.append(pltpu.make_async_copy(source, out_ref.at[to, :], sems.at[slot]))
    for copy in copies:
        copy.start()
    for copy in copies:
        copy.wait()


def collect(place, pieces):
    rows, columns = pieces[0].shape
    n = len(pieces)
    return pl.pallas_call(
        collect_body,
        out_shape=jax.ShapeDtypeStruct((n * rows, columns), BF16),
        grid_spec=pltpu.PrefetchScalarGridSpec(
            num_scalar_prefetch=1,
            grid=(1,),
            in_specs=[pl.BlockSpec((rows, columns), lambda i, place: (0, 0))] * n,
            out_specs=pl.BlockSpec(memory_space=pl.ANY),
            scratch_shapes=[pltpu.SemaphoreType.DMA((2 * n,))],
        ),
        compiler_params=params(16),
        cost_estimate=cost(MIB, 12 * MIB),
        name="collect",
    )(place, *pieces)


def back_body(place_ref, mkv_ref, mq_ref, tkv_ref, tq_ref, wm_ref, wt_ref, out_ref):
    def block(i, rows):
        source = pl.ds(pl.multiple_of(place_ref[i] * 512, 512), 512)
        out_ref[rows, :] = (
            dot(wm_ref[source, :512], mkv_ref[...], NN)
            + dot(wm_ref[source, 512:], mq_ref[...], NN)
            + dot(wt_ref[source, :512], tkv_ref[...], NN)
            + dot(wt_ref[source, 512:], tq_ref[...], NN)
        )

    over_rows(out_ref.shape[0], 512, block)


def back(place, dkvt, dqt, theirs_kv, theirs_q, w_mine, w_theirs):
    tok = dkvt.shape[1]
    depth = w_mine.shape[1]
    columns = 512 * place.shape[0]
    return pl.pallas_call(
        back_body,
        in_specs=[SMEM] + [VMEM] * 6,
        out_specs=VMEM,
        out_shape=jax.ShapeDtypeStruct((columns, tok), F32),
        compiler_params=params(),
        cost_estimate=cost(4 * tok * columns * depth, 8 * MIB),
        name="back",
    )(place, dkvt, dqt, theirs_kv, theirs_q, w_mine, w_theirs)


def turn_body(core_ref, own_ref, a_ref, b_ref, keep_ref, give_ref):
    core = core_ref[0]
    size = keep_ref.shape[0]
    mine = pl.ds(pl.multiple_of(core * size, size), size)
    theirs = pl.ds(pl.multiple_of((1 - core) * size, size), size)
    for tokens, ref in ((theirs, give_ref), (mine, keep_ref)):
        total = own_ref[:, tokens] + a_ref[:, tokens].astype(F32) + b_ref[:, tokens].astype(F32)
        ref[...] = total.astype(BF16).T


def turn(core, own, a, b):
    columns, tok = own.shape
    part = jax.ShapeDtypeStruct((tok // 2, columns), BF16)
    return pl.pallas_call(
        turn_body,
        in_specs=[SMEM] + [VMEM] * 3,
        out_specs=[VMEM] * 2,
        out_shape=[part, part],
        compiler_params=params(),
        cost_estimate=cost(4 * MIB, 6 * MIB),
        name="turn",
    )(core, own, a, b)


def join_body(core_ref, keep_ref, got_ref, out_ref):
    core = core_ref[0]
    size = keep_ref.shape[1]
    out_ref[:, pl.ds(pl.multiple_of(core * size, size), size)] = keep_ref[...]
    out_ref[:, pl.ds(pl.multiple_of((1 - core) * size, size), size)] = got_ref[...]


def join(core, keep, got):
    rows, columns = keep.shape
    return pl.pallas_call(
        join_body,
        in_specs=[SMEM] + [VMEM] * 2,
        out_specs=VMEM,
        out_shape=jax.ShapeDtypeStruct((rows, 2 * columns), BF16),
        compiler_params=params(),
        cost_estimate=cost(MIB, 2 * MIB),
        name="join",
    )(core, keep, got)


def swap(a):
    return lax.ppermute(a, "c", SWAP)


def along(a, by, inner):
    pairs = []
    for z in range(4):
        for y in range(4):
            for c in range(2):
                over_y = (c == 0) == inner
                to = (z, (y + by) % 4) if over_y else ((z + by) % 4, y)
                pairs.append(((z * 4 + y) * 2 + c, (to[0] * 4 + to[1]) * 2 + c))
    return lax.ppermute(a, ("z", "y", "c"), pairs)


def across(a, by):
    pairs = [
        (4 * c + x, 4 * c + (x + (by if c == 0 else -by)) % 4) for c in range(2) for x in range(4)
    ]
    return lax.ppermute(a, ("c", "x"), pairs)


def gather_ring(a):
    half = a.shape[0] // 2
    before = along(a, 1, True)
    after = along(a, -1, True)
    top = along(before[:half], 1, True)
    bottom = along(after[half:], -1, True)
    return a, after, top, bottom, before


def gather_halves(top, bottom):
    top3 = along(top, 1, False)
    bottom1 = along(bottom, -1, False)
    bottom3 = along(bottom, 1, False)
    top1 = along(top, -1, False)
    top2 = along(top3, 1, False)
    bottom2 = along(bottom1, -1, False)
    return (top, bottom), (top1, bottom1), (top2, bottom2), (top3, bottom3)


def scatter_ring(far, after, before, send):
    far = far.astype(BF16)
    half = far.shape[0] // 2
    top = send(far[:half], 1).astype(F32)
    bottom = send(far[half:], -1).astype(F32)
    after_plain = send(after[half:].astype(BF16), 1)
    before_plain = send(before[:half].astype(BF16), -1)
    after_sum = send((after[:half] + top).astype(BF16), 1)
    before_sum = send((before[half:] + bottom).astype(BF16), -1)
    return (after_sum, after_plain), (before_plain, before_sum)


def scatter_small(part):
    far = part(2).astype(BF16)
    half = far.shape[0] // 2
    top = along(far[:half], 1, True).astype(F32)
    bottom = along(far[half:], -1, True).astype(F32)
    after, before = part(1), part(3)
    after = jnp.concatenate([after[:half] + top, after[half:]], 0).astype(BF16)
    before = jnp.concatenate([before[:half], before[half:] + bottom], 0).astype(BF16)
    after = along(after, 1, True).astype(F32)
    before = along(before, -1, True).astype(F32)
    return part(0) + after + before


def scan_flags(inner, outer, direction):
    inner = inner if direction == 1 else 3 - inner
    outer = outer if direction == 1 else 3 - outer
    return tuple((inner >= by, outer + by > 3) for by in (1, 3, 2))


def scan_chips(state, first, flags, direction):
    near = [along(state, direction * by, True).astype(F32) for by in (1, 3, 2)]
    own = state.astype(F32)
    ahead = jnp.zeros_like(own)
    for (passed, _), a in zip(flags, near):
        ahead = ahead + jnp.where(passed, a, 0.0)
    every = near[0] + near[1] + near[2] + own
    straight = jnp.where(first, every, ahead + own).astype(BF16)
    wrapped = jnp.where(first, 0.0, ahead).astype(BF16)
    total = ahead
    for by, (_, wraps) in zip((1, 3, 2), flags):
        message = jnp.where(wraps, wrapped, straight)
        total = total + along(message, direction * by, False).astype(F32)
    return total


def in_order(first, mine, theirs, axis=0):
    one = jnp.where(first, mine, theirs)
    two = jnp.where(first, theirs, mine)
    return jnp.concatenate([one, two], axis)


def half_of(first, a, axis):
    size = a.shape[axis] // 2
    low = lax.slice_in_dim(a, 0, size, axis=axis)
    high = lax.slice_in_dim(a, size, 2 * size, axis=axis)
    return jnp.where(first, low, high), jnp.where(first, high, low)


def per_device(tokens, w_query, w_key, w_value, omega_seed, grad_out):
    core, x, y, z = (lax.axis_index(name).astype(jnp.int32) for name in ("c", "x", "y", "z"))
    outer, inner = jnp.where(core == 0, z, y), jnp.where(core == 0, y, z)
    step = jnp.arange(4, dtype=jnp.int32)
    along_outer, along_inner = (outer + step) % 4, (inner + step) % 4
    chip = jnp.where(
        core == 0,
        along_outer[:, None] * 4 + along_inner[None, :],
        along_inner[None, :] * 4 + along_outer[:, None],
    ).reshape(16)

    way = 1 - 2 * core

    def place_of(*steps):
        return jnp.stack([2 * ((x + way * by) % 4) + core for by in steps])

    where = (
        core == 0,
        jnp.concatenate([chip, core[None]]),
        chip,
        core[None],
        place_of(2),
        place_of(1, -1),
        place_of(0),
        scan_flags(inner, outer, 1),
        scan_flags(inner, outer, -1),
    )
    where, tokens, w_query, w_key, w_value, omega_seed, grad_out = lax.optimization_barrier(
        (where, tokens, w_query, w_key, w_value, omega_seed, grad_out)
    )
    first, idx, chip, core, far_place, side_place, own_place, ahead_flags, behind_flags = where

    w_mine, w_give = halve(core, (w_key, w_value, w_query))
    w_chip = in_order(first, w_mine, swap(w_give))
    g_got = swap(grad_out)
    g = in_order(first, half_of(first, grad_out, 1)[0], half_of(first, g_got, 1)[0])
    other = swap(tokens)
    seed = half_of(first, omega_seed, 0)[0].astype(BF16)

    w0, w1, w2_top, w2_bottom, w3 = gather_ring(w_chip)
    w_groups = gather_halves(
        jnp.concatenate([w0, w1], 0), jnp.concatenate([w2_top, w2_bottom, w3], 0)
    )
    arranged = [arrange(idx, tokens, other, a) for a in range(4)]
    xs = [a[0] for a in arranged]
    acc = project(first_body, [], [xs[0]], list(w_groups[0]), F32)
    pieces = list(w_groups[1] + w_groups[3])
    acc = project(more_body, [acc], [xs[1], xs[3]], pieces, F32)
    top, bottom = w_groups[2]
    acc = project(top_body, [acc], [xs[2]], [top], F32)
    kvq = project(end_body, [acc], [xs[2]], [bottom], BF16)

    kf, before, total = keys_stage(kvq, seed)
    prefix = scan_chips(total, first, ahead_flags, 1)
    weights = collect(chip, [p for pair in w_groups for p in pair])
    weights_theirs = swap(weights)
    qf, s, num, den = local_stage(kvq, kf, seed, before)
    gn, gd, later = ratio_stage(qf, num, den, g, prefix)
    suffix = scan_chips(later, first, behind_flags, -1)
    dq, dqt, dkf, dv = middle_stage(kvq, kf, qf, s, gn, gd, seed, before, prefix)
    dkv, dkvt = last_stage(kvq, kf, dkf, dv, seed, suffix)

    theirs_q = swap(dqt)
    theirs_kv = swap(dkvt)

    def group(a):
        x_rows = arranged[a][1]
        early = wgrad_call(early_body, x_rows, dq, [], 256)
        return wgrad_call(wgrad_body, x_rows, dkv, [early], 768)

    def quarters(place):
        return back(place, dkvt, dqt, theirs_kv, theirs_q, weights, weights_theirs)

    after, before = scatter_ring(group(2), group(1), group(3), lambda a, by: along(a, by, False))
    own = group(0)
    half = own.shape[0] // 2
    row_sum = [
        own[i * half : (i + 1) * half] + after[i].astype(F32) + before[i].astype(F32)
        for i in range(2)
    ]

    def strip_of(b):
        size = half // 2
        return row_sum[b // 2][b % 2 * size : (b % 2 + 1) * size]

    total_w = scatter_small(strip_of).astype(BF16)

    far = across(quarters(far_place).astype(BF16), 1)
    sides = quarters(side_place)
    size = sides.shape[0] // 2
    plain = across(sides[size:].astype(BF16), -1)
    summed = across((sides[:size] + far.astype(F32)).astype(BF16), 1)
    input_keep, input_give = turn(core, quarters(own_place), plain, summed)
    input_grad = join(core, input_keep, swap(input_give))

    keep, give = half_of(first, total_w, 0)
    return input_grad, *finish(core, keep, swap(give))


def solution(mesh):
    chips = Mesh(mesh.devices.reshape(4, 4, 2, 4), ("z", "y", "c", "x"))
    seq = ("z", "y", "c")
    placed = (
        P(seq, None),
        P(seq, "x"),
        P(seq, "x"),
        P(seq, "x"),
        P("x", None, None),
        P(seq, "x"),
    )
    specs = (P(seq, "x"), P(seq, "x"), P(seq, "x"), P(seq, "x"))

    return jax.shard_map(per_device, mesh=chips, in_specs=placed, out_specs=specs, check_vma=False)
```

```python
import math

import jax
import jax.numpy as jnp
from jax import lax
from jax.experimental import pallas as pl
from jax.experimental.pallas import tpu as pltpu
from jax.sharding import Mesh, PartitionSpec as P


F32 = jnp.float32
BF16 = jnp.bfloat16
SEED_STEP = 0.4
CHUNK = 256
NT = (((1,), (1,)), ((), ()))
TN = (((0,), (0,)), ((), ()))
NN = (((1,), (0,)), ((), ()))
SWAP = ((0, 1), (1, 0))
STATE_ROWS = 136
SENT_ROWS = 272
MIB = 1 << 20


def dot(a, b, dims):
    return lax.dot_general(a, b, dims, preferred_element_type=F32)


GRANT = 12


VMEM = pl.BlockSpec(memory_space=pltpu.VMEM)
SMEM = pl.BlockSpec(memory_space=pltpu.SMEM)


def over_rows(count, size, body):
    def step(i, _):
        body(i, pl.ds(pl.multiple_of(i * size, size), size))

    lax.fori_loop(0, count // size, step, None)


def params(vmem=GRANT):
    return pltpu.CompilerParams(vmem_limit_bytes=vmem * MIB)


def cost(flops, nbytes):
    return pl.CostEstimate(flops=flops, bytes_accessed=nbytes, transcendentals=0)


def halve_body(core_ref, *refs):
    *sources, mine_ref, give_ref = refs
    core = core_ref[0]
    half = sources[0].shape[1] // 2
    mine = pl.ds(pl.multiple_of(core * half, half), half)
    give = pl.ds(pl.multiple_of((1 - core) * half, half), half)
    for i, ref in enumerate(sources):
        cols = slice(half * i, half * i + half)
        mine_ref[:, cols] = ref[:, mine]
        give_ref[:, cols] = ref[:, give]


def halve(core, sources):
    size, columns = sources[0].shape
    whole = pl.BlockSpec((size, columns), lambda i, core: (0, 0))
    shape = (size, len(sources) * columns // 2)
    return pl.pallas_call(
        halve_body,
        out_shape=[jax.ShapeDtypeStruct(shape, BF16)] * 2,
        grid_spec=pltpu.PrefetchScalarGridSpec(
            num_scalar_prefetch=1,
            grid=(1,),
            in_specs=[whole] * len(sources),
            out_specs=[pl.BlockSpec(shape, lambda i, core: (0, 0))] * 2,
        ),
        compiler_params=params(56),
        cost_estimate=cost(MIB, MIB),
        name="halve",
    )(core, *sources)


def arrange_body(idx_ref, own_ref, other_ref, rows_ref, columns_ref):
    core = idx_ref[16]
    size = own_ref.shape[0]
    mine = pl.ds(pl.multiple_of(core * size, size), size)
    theirs = pl.ds(pl.multiple_of((1 - core) * size, size), size)
    own, other = own_ref[...], other_ref[...]
    rows_ref[mine, :] = own
    rows_ref[theirs, :] = other
    columns_ref[:, mine] = own.T
    columns_ref[:, theirs] = other.T


def arrange(idx, own, other, group):
    size, depth = own.shape
    width = depth // 16
    source = pl.BlockSpec((size, width), lambda k, idx: (0, idx[4 * group + k]))
    return pl.pallas_call(
        arrange_body,
        out_shape=[
            jax.ShapeDtypeStruct((2 * size, 4 * width), BF16),
            jax.ShapeDtypeStruct((4 * width, 2 * size), BF16),
        ],
        grid_spec=pltpu.PrefetchScalarGridSpec(
            num_scalar_prefetch=1,
            grid=(4,),
            in_specs=[source, source],
            out_specs=[
                pl.BlockSpec((2 * size, width), lambda k, idx: (0, k)),
                pl.BlockSpec((width, 2 * size), lambda k, idx: (k, 0)),
            ],
        ),
        compiler_params=params(),
        cost_estimate=cost(4 * MIB, 6 * MIB),
        name="arrange",
    )(idx, own, other)


def halves_dot(x_ref, rows, wa_ref, wb_ref):
    half = wa_ref.shape[0]
    return dot(x_ref[rows, :half], wa_ref[...], NN) + dot(x_ref[rows, half:], wb_ref[...], NN)


def first_body(x_ref, wa_ref, wb_ref, out_ref):
    def block(_, rows):
        out_ref[rows, :] = halves_dot(x_ref, rows, wa_ref, wb_ref)

    over_rows(out_ref.shape[0], CHUNK, block)


def more_body(acc_ref, xa_ref, xb_ref, *rest):
    *w_refs, out_ref = rest

    def block(_, rows):
        total = acc_ref[rows, :]
        for x_ref, pair in ((xa_ref, w_refs[:2]), (xb_ref, w_refs[2:])):
            total += halves_dot(x_ref, rows, *pair)
        out_ref[rows, :] = total

    over_rows(out_ref.shape[0], CHUNK, block)


def top_body(acc_ref, x_ref, w_ref, out_ref):
    def block(_, rows):
        out_ref[rows, :] = acc_ref[rows, :] + dot(x_ref[rows, : w_ref.shape[0]], w_ref[...], NN)

    over_rows(out_ref.shape[0], CHUNK, block)


def end_body(acc_ref, x_ref, w_ref, out_ref):
    def block(_, rows):
        out = acc_ref[rows, :] + dot(x_ref[rows, w_ref.shape[0] :], w_ref[...], NN)
        out_ref[rows, :] = out.astype(BF16)

    over_rows(out_ref.shape[0], CHUNK, block)


def project(body, acc, xs, ws, dtype):
    tok = xs[0].shape[0]
    columns = ws[0].shape[1]
    ops = acc + xs + ws
    depth = sum(w.shape[0] for w in ws)
    return pl.pallas_call(
        body,
        in_specs=[VMEM] * len(ops),
        out_specs=VMEM,
        out_shape=jax.ShapeDtypeStruct((tok, columns), dtype),
        compiler_params=params(),
        cost_estimate=cost(2 * tok * depth * columns, 8 * MIB),
    )(*ops)


def features(rows, seed):
    size = rows.shape[1]
    scale = size ** (-0.25)
    scaled = rows.astype(F32) * scale
    projected = dot(rows, seed, NN) * (SEED_STEP * scale)
    norm = 0.5 * jnp.sum(scaled * scaled, -1, keepdims=True)
    return jnp.exp(projected - norm) * (1.0 / math.sqrt(seed.shape[1]))


def feature_grad(weighted, rows, seed):
    scale = rows.shape[1] ** (-0.25)
    projected = dot(weighted.astype(BF16), seed, NT) * SEED_STEP
    total = jnp.sum(weighted, -1, keepdims=True)
    return (projected - total * (rows.astype(F32) * scale)) * scale


def send_state(ref, carry_ref):
    for head in range(2):
        ref[128 * head : 128 * head + 128, :] = carry_ref[head, :128, :].astype(BF16)
    rest = jnp.zeros((SENT_ROWS - 258, 256), F32)
    sums = [carry_ref[0, 128:129, :], carry_ref[1, 128:129, :], rest]
    ref[256:, :] = jnp.concatenate(sums, 0).astype(BF16)


def state_of(ref, head):
    return ref[128 * head : 128 * head + 128, :], ref[256 + head : 257 + head, :]


def mask_of(size):
    return lax.broadcasted_iota(jnp.int32, (size, size), 0) >= lax.broadcasted_iota(
        jnp.int32, (size, size), 1
    )


PER_STEP = 2


def over_chunks(n, body):
    def step(i, _):
        for part in range(PER_STEP):
            start = (i * PER_STEP + part) * CHUNK
            body(i * PER_STEP + part, pl.ds(pl.multiple_of(start, CHUNK), CHUNK))

    lax.fori_loop(0, n // PER_STEP, step, None)


def keys_body(kvq_ref, seed_ref, kf_ref, before_ref, total_ref, carry_ref):
    carry_ref[...] = jnp.zeros_like(carry_ref)
    pad = jnp.zeros((STATE_ROWS - 129, 256), F32)

    def chunk(i, rows):
        for head in range(2):
            state = carry_ref[head]
            before_ref[i, head] = state
            kf = features(kvq_ref[rows, 128 * head : 128 * head + 128], seed_ref[head])
            kf = kf.astype(BF16)
            kf_ref[rows, 256 * head : 256 * head + 256] = kf
            main = dot(kvq_ref[rows, 256 + 128 * head : 384 + 128 * head], kf, TN)
            row = jnp.sum(kf.astype(F32), 0, keepdims=True)
            carry_ref[head] = state + jnp.concatenate([main, row, pad], 0)

    over_chunks(kvq_ref.shape[0] // CHUNK, chunk)
    send_state(total_ref, carry_ref)


def keys_stage(kvq, seed):
    tok = kvq.shape[0]
    n = tok // CHUNK
    state = (2, STATE_ROWS, 256)
    return pl.pallas_call(
        keys_body,
        in_specs=[VMEM] * 2,
        out_specs=[VMEM] * 3,
        out_shape=[
            jax.ShapeDtypeStruct((tok, 512), BF16),
            jax.ShapeDtypeStruct((n,) + state, F32),
            jax.ShapeDtypeStruct((SENT_ROWS, 256), BF16),
        ],
        scratch_shapes=[pltpu.VMEM(state, F32)],
        compiler_params=params(),
        cost_estimate=cost(n * 2 * 4 * 256 * 256 * 128, 4 * MIB),
        name="keys_stage",
    )(kvq, seed)


def local_body(q_ref, v_ref, kf_ref, seed_ref, before_ref, qf_ref, s_ref, num_ref, den_ref):
    mask = mask_of(CHUNK)
    for head in range(2):
        cols = slice(128 * head, 128 * head + 128)
        wide = slice(256 * head, 256 * head + 256)
        qf = features(q_ref[:, cols], seed_ref[head]).astype(BF16)
        qf_ref[:, wide] = qf
        scores = jnp.where(mask, dot(qf, kf_ref[:, wide], NT), 0.0)
        s16 = scores.astype(BF16)
        s_ref[:, wide] = s16
        main = before_ref[0, head, :128, :].astype(BF16)
        row = before_ref[0, head, 128:129, :]
        num_ref[:, cols] = dot(s16, v_ref[:, cols], NN) + dot(qf, main, NT)
        den_ref[head] = jnp.sum(scores, -1, keepdims=True) + jnp.sum(
            qf.astype(F32) * row, -1, keepdims=True
        )


def local_stage(kvq, kf, seed, before):
    tok = kvq.shape[0]
    n = tok // CHUNK
    return pl.pallas_call(
        local_body,
        grid=(n,),
        in_specs=[
            pl.BlockSpec((CHUNK, 256), lambda i: (i, 2)),
            pl.BlockSpec((CHUNK, 256), lambda i: (i, 1)),
            pl.BlockSpec((CHUNK, 512), lambda i: (i, 0)),
            pl.BlockSpec((2, 128, 256), lambda i: (0, 0, 0)),
            pl.BlockSpec((1, 2, STATE_ROWS, 256), lambda i: (i, 0, 0, 0)),
        ],
        out_specs=[
            pl.BlockSpec((CHUNK, 512), lambda i: (i, 0)),
            pl.BlockSpec((CHUNK, 512), lambda i: (i, 0)),
            pl.BlockSpec((CHUNK, 256), lambda i: (i, 0)),
            pl.BlockSpec((2, CHUNK, 1), lambda i: (0, i, 0)),
        ],
        out_shape=[
            jax.ShapeDtypeStruct((tok, 512), BF16),
            jax.ShapeDtypeStruct((tok, 512), BF16),
            jax.ShapeDtypeStruct((tok, 256), F32),
            jax.ShapeDtypeStruct((2, tok, 1), F32),
        ],
        compiler_params=params(),
        cost_estimate=cost(n * 2 * 10 * 256 * 256 * 128, 6 * MIB),
        name="local_stage",
    )(kvq, kvq, kf, seed, before)


def ratio_body(qf_ref, num_ref, den_ref, g_ref, prefix_ref, gn_ref, gd_ref, total_ref, carry_ref):
    carry_ref[...] = jnp.zeros_like(carry_ref)

    def chunk(i, rows):
        for head in range(2):
            cols = slice(128 * head, 128 * head + 128)
            main, row = state_of(prefix_ref, head)
            main = main.astype(BF16)
            qf = qf_ref[rows, 256 * head : 256 * head + 256]
            qf32 = qf.astype(F32)
            num = num_ref[rows, cols] + dot(qf, main, NT)
            den = den_ref[head, rows] + jnp.sum(qf32 * row, -1, keepdims=True)
            inverse = 1.0 / den
            g = g_ref[rows, cols].astype(F32)
            gn = (g * inverse).astype(BF16)
            gd = -jnp.sum(g * num, -1, keepdims=True) * inverse * inverse
            gn_ref[rows, cols] = gn
            gd_ref[head, rows] = gd
            carry_ref[head, :128, :] += dot(gn, qf, TN)
            carry_ref[head, 128:129, :] += jnp.sum(qf32 * gd, 0, keepdims=True)

    over_chunks(qf_ref.shape[0] // CHUNK, chunk)
    send_state(total_ref, carry_ref)


def ratio_stage(qf, num, den, g, prefix):
    tok = qf.shape[0]
    n = tok // CHUNK
    state = (2, STATE_ROWS, 256)
    return pl.pallas_call(
        ratio_body,
        in_specs=[VMEM] * 5,
        out_specs=[VMEM] * 3,
        out_shape=[
            jax.ShapeDtypeStruct((tok, 256), BF16),
            jax.ShapeDtypeStruct((2, tok, 1), F32),
            jax.ShapeDtypeStruct((SENT_ROWS, 256), BF16),
        ],
        scratch_shapes=[pltpu.VMEM(state, F32)],
        compiler_params=params(),
        cost_estimate=cost(n * 2 * 4 * 256 * 256 * 128, 4 * MIB),
        name="ratio_stage",
    )(qf, num, den, g, prefix)


def middle_body(
    q_ref, v_ref, kf_ref, qf_ref, s_ref, gn_ref, gd_ref, seed_ref, before_ref, prefix_ref,
    dq_ref, dqt_ref, dkf_ref, dv_ref, carry_ref,
):
    step = pl.program_id(0)
    mask = mask_of(CHUNK)

    @pl.when(step == 0)
    def _():
        carry_ref[...] = jnp.zeros_like(carry_ref)

    for head in range(2):
        cols = slice(128 * head, 128 * head + 128)
        wide = slice(256 * head, 256 * head + 256)
        qf, kf, gn, gd = qf_ref[:, wide], kf_ref[:, wide], gn_ref[:, cols], gd_ref[head]
        v = v_ref[:, cols]
        qf32 = qf.astype(F32)
        pairs = jnp.where(mask, dot(gn, v, NT) + gd, 0.0).astype(BF16)
        main, row = state_of(prefix_ref, head)
        main = (main + before_ref[0, head, :128, :]).astype(BF16)
        row = row + before_ref[0, head, 128:129, :]
        dqf = dot(pairs, kf, NN) + dot(gn, main, NN) + gd * row
        dq = feature_grad(dqf * qf32, q_ref[:, cols], seed_ref[head]).astype(BF16)
        dq_ref[:, cols] = dq
        dqt_ref[cols, :] = dq.T
        later = carry_ref[head]
        later_main, later_row = later[:128].astype(BF16), later[128:129]
        dkf_ref[:, wide] = dot(pairs, qf, TN) + dot(v, later_main, NN) + later_row
        dv_ref[:, cols] = dot(s_ref[:, wide], gn, TN) + dot(kf, later_main, NT)
        carry_ref[head, :128, :] += dot(gn, qf, TN)
        carry_ref[head, 128:129, :] += jnp.sum(qf32 * gd, 0, keepdims=True)


def middle_stage(kvq, kf, qf, s, gn, gd, seed, before, prefix):
    tok = qf.shape[0]
    n = tok // CHUNK
    state = (2, STATE_ROWS, 256)

    def narrow(column):
        return pl.BlockSpec((CHUNK, 256), lambda i: (n - 1 - i, column))

    wide = pl.BlockSpec((CHUNK, 512), lambda i: (n - 1 - i, 0))
    return pl.pallas_call(
        middle_body,
        grid=(n,),
        in_specs=[
            narrow(2), narrow(1), wide, wide, wide, narrow(0),
            pl.BlockSpec((2, CHUNK, 1), lambda i: (0, n - 1 - i, 0)),
            pl.BlockSpec((2, 128, 256), lambda i: (0, 0, 0)),
            pl.BlockSpec((1,) + state, lambda i: (n - 1 - i, 0, 0, 0)),
            pl.BlockSpec((SENT_ROWS, 256), lambda i: (0, 0)),
        ],
        out_specs=[
            narrow(0),
            pl.BlockSpec((256, CHUNK), lambda i: (0, n - 1 - i)),
            wide,
            narrow(0),
        ],
        out_shape=[
            jax.ShapeDtypeStruct((tok, 256), BF16),
            jax.ShapeDtypeStruct((256, tok), BF16),
            jax.ShapeDtypeStruct((tok, 512), F32),
            jax.ShapeDtypeStruct((tok, 256), F32),
        ],
        scratch_shapes=[pltpu.VMEM(state, F32)],
        compiler_params=params(),
        cost_estimate=cost(n * 2 * 20 * 256 * 256 * 128, 10 * MIB),
        name="middle_stage",
    )(kvq, kvq, kf, qf, s, gn, gd, seed, before, prefix)


def last_body(kvq_ref, kf_ref, dkf_ref, dv_ref, seed_ref, suffix_ref, out_ref, outt_ref):
    def chunk(i, rows):
        for head in range(2):
            cols = slice(128 * head, 128 * head + 128)
            wide = slice(256 * head, 256 * head + 256)
            dv_cols = slice(256 + 128 * head, 384 + 128 * head)
            main, row = state_of(suffix_ref, head)
            main = main.astype(BF16)
            kf = kf_ref[rows, wide]
            dkf = dkf_ref[rows, wide] + dot(kvq_ref[rows, dv_cols], main, NN) + row
            dk = feature_grad(dkf * kf.astype(F32), kvq_ref[rows, cols], seed_ref[head])
            dk = dk.astype(BF16)
            dv = (dv_ref[rows, cols] + dot(kf, main, NT)).astype(BF16)
            out_ref[rows, cols] = dk
            out_ref[rows, dv_cols] = dv
            outt_ref[cols, rows] = dk.T
            outt_ref[dv_cols, rows] = dv.T

    over_chunks(kvq_ref.shape[0] // CHUNK, chunk)


def last_stage(kvq, kf, dkf, dv, seed, suffix):
    tok = kf.shape[0]
    n = tok // CHUNK
    return pl.pallas_call(
        last_body,
        in_specs=[VMEM] * 6,
        out_specs=[VMEM] * 2,
        out_shape=[
            jax.ShapeDtypeStruct((tok, 512), BF16),
            jax.ShapeDtypeStruct((512, tok), BF16),
        ],
        compiler_params=params(),
        cost_estimate=cost(n * 2 * 6 * 256 * 256 * 128, 6 * MIB),
        name="last_stage",
    )(kvq, kf, dkf, dv, seed, suffix)


def early_body(x_ref, d_ref, out_ref):
    def block(_, rows):
        out_ref[rows, :] = dot(x_ref[rows, :], d_ref[...], NN)

    over_rows(out_ref.shape[0], 512, block)


def wgrad_body(x_ref, dkv_ref, early_ref, out_ref):
    def block(_, rows):
        out_ref[rows, :512] = dot(x_ref[rows, :], dkv_ref[...], NN)
        out_ref[rows, 512:] = early_ref[rows, :]

    over_rows(out_ref.shape[0], 512, block)


def wgrad_call(body, x, d, early, columns):
    depth, tok = x.shape
    return pl.pallas_call(
        body,
        in_specs=[VMEM] * (2 + len(early)),
        out_specs=VMEM,
        out_shape=jax.ShapeDtypeStruct((depth, columns), F32),
        compiler_params=params(),
        cost_estimate=cost(2 * tok * depth * columns, 6 * MIB),
    )(x, d, *early)


def finish_body(core_ref, keep_ref, got_ref, q_ref, k_ref, v_ref):
    core = core_ref[0]
    mine = pl.ds(pl.multiple_of(core * 256, 256), 256)
    theirs = pl.ds(pl.multiple_of((1 - core) * 256, 256), 256)
    for place, ref in enumerate((k_ref, v_ref, q_ref)):
        cols = slice(256 * place, 256 * place + 256)
        ref[:, mine] = keep_ref[:, cols].astype(F32)
        ref[:, theirs] = got_ref[:, cols].astype(F32)


def finish(core, keep, got):
    rows = keep.shape[0]
    out = jax.ShapeDtypeStruct((rows, 512), F32)
    whole = pl.BlockSpec(keep.shape, lambda i, core: (0, 0))
    return pl.pallas_call(
        finish_body,
        out_shape=[out] * 3,
        grid_spec=pltpu.PrefetchScalarGridSpec(
            num_scalar_prefetch=1,
            grid=(1,),
            in_specs=[whole, whole],
            out_specs=[pl.BlockSpec((rows, 512), lambda i, core: (0, 0))] * 3,
        ),
        compiler_params=params(8),
        cost_estimate=cost(MIB, MIB),
        name="finish",
    )(core, keep, got)


def collect_body(place_ref, *refs):
    *pieces, out_ref, sems = refs
    size = pieces[0].shape[0] // 2
    copies = []
    for slot in range(2 * len(pieces)):
        to = pl.ds(pl.multiple_of(place_ref[slot] * size, size), size)
        source = pieces[slot // 2].at[pl.ds(slot % 2 * size, size), :]
        copies.append(pltpu.make_async_copy(source, out_ref.at[to, :], sems.at[slot]))
    for copy in copies:
        copy.start()
    for copy in copies:
        copy.wait()


def collect(place, pieces):
    rows, columns = pieces[0].shape
    n = len(pieces)
    return pl.pallas_call(
        collect_body,
        out_shape=jax.ShapeDtypeStruct((n * rows, columns), BF16),
        grid_spec=pltpu.PrefetchScalarGridSpec(
            num_scalar_prefetch=1,
            grid=(1,),
            in_specs=[pl.BlockSpec((rows, columns), lambda i, place: (0, 0))] * n,
            out_specs=pl.BlockSpec(memory_space=pl.ANY),
            scratch_shapes=[pltpu.SemaphoreType.DMA((2 * n,))],
        ),
        compiler_params=params(16),
        cost_estimate=cost(MIB, 12 * MIB),
        name="collect",
    )(place, *pieces)


def back_body(place_ref, mkv_ref, mq_ref, tkv_ref, tq_ref, wm_ref, wt_ref, out_ref):
    def block(i, rows):
        source = pl.ds(pl.multiple_of(place_ref[i] * 512, 512), 512)
        out_ref[rows, :] = (
            dot(wm_ref[source, :512], mkv_ref[...], NN)
            + dot(wm_ref[source, 512:], mq_ref[...], NN)
            + dot(wt_ref[source, :512], tkv_ref[...], NN)
            + dot(wt_ref[source, 512:], tq_ref[...], NN)
        )

    over_rows(out_ref.shape[0], 512, block)


def back(place, dkvt, dqt, theirs_kv, theirs_q, w_mine, w_theirs):
    tok = dkvt.shape[1]
    depth = w_mine.shape[1]
    columns = 512 * place.shape[0]
    return pl.pallas_call(
        back_body,
        in_specs=[SMEM] + [VMEM] * 6,
        out_specs=VMEM,
        out_shape=jax.ShapeDtypeStruct((columns, tok), F32),
        compiler_params=params(),
        cost_estimate=cost(4 * tok * columns * depth, 8 * MIB),
        name="back",
    )(place, dkvt, dqt, theirs_kv, theirs_q, w_mine, w_theirs)


def turn_body(core_ref, own_ref, a_ref, b_ref, keep_ref, give_ref):
    core = core_ref[0]
    size = keep_ref.shape[0]
    mine = pl.ds(pl.multiple_of(core * size, size), size)
    theirs = pl.ds(pl.multiple_of((1 - core) * size, size), size)
    for tokens, ref in ((theirs, give_ref), (mine, keep_ref)):
        total = own_ref[:, tokens] + a_ref[:, tokens].astype(F32) + b_ref[:, tokens].astype(F32)
        ref[...] = total.astype(BF16).T


def turn(core, own, a, b):
    columns, tok = own.shape
    part = jax.ShapeDtypeStruct((tok // 2, columns), BF16)
    return pl.pallas_call(
        turn_body,
        in_specs=[SMEM] + [VMEM] * 3,
        out_specs=[VMEM] * 2,
        out_shape=[part, part],
        compiler_params=params(),
        cost_estimate=cost(4 * MIB, 6 * MIB),
        name="turn",
    )(core, own, a, b)


def join_body(core_ref, keep_ref, got_ref, out_ref):
    core = core_ref[0]
    size = keep_ref.shape[1]
    out_ref[:, pl.ds(pl.multiple_of(core * size, size), size)] = keep_ref[...]
    out_ref[:, pl.ds(pl.multiple_of((1 - core) * size, size), size)] = got_ref[...]


def join(core, keep, got):
    rows, columns = keep.shape
    return pl.pallas_call(
        join_body,
        in_specs=[SMEM] + [VMEM] * 2,
        out_specs=VMEM,
        out_shape=jax.ShapeDtypeStruct((rows, 2 * columns), BF16),
        compiler_params=params(),
        cost_estimate=cost(MIB, 2 * MIB),
        name="join",
    )(core, keep, got)


def swap(a):
    return lax.ppermute(a, "c", SWAP)


def along(a, by, inner):
    pairs = []
    for z in range(4):
        for y in range(4):
            for c in range(2):
                over_y = (c == 0) == inner
                to = (z, (y + by) % 4) if over_y else ((z + by) % 4, y)
                pairs.append(((z * 4 + y) * 2 + c, (to[0] * 4 + to[1]) * 2 + c))
    return lax.ppermute(a, ("z", "y", "c"), pairs)


def across(a, by):
    pairs = [
        (4 * c + x, 4 * c + (x + (by if c == 0 else -by)) % 4) for c in range(2) for x in range(4)
    ]
    return lax.ppermute(a, ("c", "x"), pairs)


def gather_ring(a):
    half = a.shape[0] // 2
    before = along(a, 1, True)
    after = along(a, -1, True)
    top = along(before[:half], 1, True)
    bottom = along(after[half:], -1, True)
    return a, after, top, bottom, before


def gather_halves(top, bottom):
    top3 = along(top, 1, False)
    bottom1 = along(bottom, -1, False)
    bottom3 = along(bottom, 1, False)
    top1 = along(top, -1, False)
    top2 = along(top3, 1, False)
    bottom2 = along(bottom1, -1, False)
    return (top, bottom), (top1, bottom1), (top2, bottom2), (top3, bottom3)


def scatter_ring(far, after, before, send):
    far = far.astype(BF16)
    half = far.shape[0] // 2
    top = send(far[:half], 1).astype(F32)
    bottom = send(far[half:], -1).astype(F32)
    after_plain = send(after[half:].astype(BF16), 1)
    before_plain = send(before[:half].astype(BF16), -1)
    after_sum = send((after[:half] + top).astype(BF16), 1)
    before_sum = send((before[half:] + bottom).astype(BF16), -1)
    return (after_sum, after_plain), (before_plain, before_sum)


def scatter_small(part):
    far = part(2).astype(BF16)
    half = far.shape[0] // 2
    top = along(far[:half], 1, True).astype(F32)
    bottom = along(far[half:], -1, True).astype(F32)
    after, before = part(1), part(3)
    after = jnp.concatenate([after[:half] + top, after[half:]], 0).astype(BF16)
    before = jnp.concatenate([before[:half], before[half:] + bottom], 0).astype(BF16)
    after = along(after, 1, True).astype(F32)
    before = along(before, -1, True).astype(F32)
    return part(0) + after + before


def scan_flags(inner, outer, direction):
    inner = inner if direction == 1 else 3 - inner
    outer = outer if direction == 1 else 3 - outer
    return tuple((inner >= by, outer + by > 3) for by in (1, 3, 2))


def scan_chips(state, first, flags, direction):
    near = [along(state, direction * by, True).astype(F32) for by in (1, 3, 2)]
    own = state.astype(F32)
    ahead = jnp.zeros_like(own)
    for (passed, _), a in zip(flags, near):
        ahead = ahead + jnp.where(passed, a, 0.0)
    every = near[0] + near[1] + near[2] + own
    straight = jnp.where(first, every, ahead + own).astype(BF16)
    wrapped = jnp.where(first, 0.0, ahead).astype(BF16)
    total = ahead
    for by, (_, wraps) in zip((1, 3, 2), flags):
        message = jnp.where(wraps, wrapped, straight)
        total = total + along(message, direction * by, False).astype(F32)
    return total


def in_order(first, mine, theirs, axis=0):
    one = jnp.where(first, mine, theirs)
    two = jnp.where(first, theirs, mine)
    return jnp.concatenate([one, two], axis)


def half_of(first, a, axis):
    size = a.shape[axis] // 2
    low = lax.slice_in_dim(a, 0, size, axis=axis)
    high = lax.slice_in_dim(a, size, 2 * size, axis=axis)
    return jnp.where(first, low, high), jnp.where(first, high, low)


def per_device(tokens, w_query, w_key, w_value, omega_seed, grad_out):
    core, x, y, z = (lax.axis_index(name).astype(jnp.int32) for name in ("c", "x", "y", "z"))
    outer, inner = jnp.where(core == 0, z, y), jnp.where(core == 0, y, z)
    step = jnp.arange(4, dtype=jnp.int32)
    along_outer, along_inner = (outer + step) % 4, (inner + step) % 4
    chip = jnp.where(
        core == 0,
        along_outer[:, None] * 4 + along_inner[None, :],
        along_inner[None, :] * 4 + along_outer[:, None],
    ).reshape(16)

    way = 1 - 2 * core

    def place_of(*steps):
        return jnp.stack([2 * ((x + way * by) % 4) + core for by in steps])

    where = (
        core == 0,
        jnp.concatenate([chip, core[None]]),
        chip,
        core[None],
        place_of(2),
        place_of(1, -1),
        place_of(0),
        scan_flags(inner, outer, 1),
        scan_flags(inner, outer, -1),
    )
    where, tokens, w_query, w_key, w_value, omega_seed, grad_out = lax.optimization_barrier(
        (where, tokens, w_query, w_key, w_value, omega_seed, grad_out)
    )
    first, idx, chip, core, far_place, side_place, own_place, ahead_flags, behind_flags = where

    w_mine, w_give = halve(core, (w_key, w_value, w_query))
    w_chip = in_order(first, w_mine, swap(w_give))
    g_got = swap(grad_out)
    g = in_order(first, half_of(first, grad_out, 1)[0], half_of(first, g_got, 1)[0])
    other = swap(tokens)
    seed = half_of(first, omega_seed, 0)[0].astype(BF16)

    w0, w1, w2_top, w2_bottom, w3 = gather_ring(w_chip)
    w_groups = gather_halves(
        jnp.concatenate([w0, w1], 0), jnp.concatenate([w2_top, w2_bottom, w3], 0)
    )
    arranged = [arrange(idx, tokens, other, a) for a in range(4)]
    xs = [a[0] for a in arranged]
    acc = project(first_body, [], [xs[0]], list(w_groups[0]), F32)
    pieces = list(w_groups[1] + w_groups[3])
    acc = project(more_body, [acc], [xs[1], xs[3]], pieces, F32)
    top, bottom = w_groups[2]
    acc = project(top_body, [acc], [xs[2]], [top], F32)
    kvq = project(end_body, [acc], [xs[2]], [bottom], BF16)

    kf, before, total = keys_stage(kvq, seed)
    prefix = scan_chips(total, first, ahead_flags, 1)
    weights = collect(chip, [p for pair in w_groups for p in pair])
    weights_theirs = swap(weights)
    qf, s, num, den = local_stage(kvq, kf, seed, before)
    gn, gd, later = ratio_stage(qf, num, den, g, prefix)
    suffix = scan_chips(later, first, behind_flags, -1)
    dq, dqt, dkf, dv = middle_stage(kvq, kf, qf, s, gn, gd, seed, before, prefix)
    dkv, dkvt = last_stage(kvq, kf, dkf, dv, seed, suffix)

    theirs_q = swap(dqt)
    theirs_kv = swap(dkvt)

    def group(a):
        x_rows = arranged[a][1]
        early = wgrad_call(early_body, x_rows, dq, [], 256)
        return wgrad_call(wgrad_body, x_rows, dkv, [early], 768)

    def quarters(place):
        return back(place, dkvt, dqt, theirs_kv, theirs_q, weights, weights_theirs)

    after, before = scatter_ring(group(2), group(1), group(3), lambda a, by: along(a, by, False))
    own = group(0)
    half = own.shape[0] // 2
    row_sum = [
        own[i * half : (i + 1) * half] + after[i].astype(F32) + before[i].astype(F32)
        for i in range(2)
    ]

    def strip_of(b):
        size = half // 2
        return row_sum[b // 2][b % 2 * size : (b % 2 + 1) * size]

    total_w = scatter_small(strip_of).astype(BF16)

    far = across(quarters(far_place).astype(BF16), 1)
    sides = quarters(side_place)
    size = sides.shape[0] // 2
    plain = across(sides[size:].astype(BF16), -1)
    summed = across((sides[:size] + far.astype(F32)).astype(BF16), 1)
    input_keep, input_give = turn(core, quarters(own_place), plain, summed)
    input_grad = join(core, input_keep, swap(input_give))

    keep, give = half_of(first, total_w, 0)
    return input_grad, *finish(core, keep, swap(give))


def solution(mesh):
    chips = Mesh(mesh.devices.reshape(4, 4, 2, 4), ("z", "y", "c", "x"))
    seq = ("z", "y", "c")
    placed = (
        P(seq, None),
        P(seq, "x"),
        P(seq, "x"),
        P(seq, "x"),
        P("x", None, None),
        P(seq, "x"),
    )
    specs = (P(seq, "x"), P(seq, "x"), P(seq, "x"), P(seq, "x"))

    return jax.shard_map(per_device, mesh=chips, in_specs=placed, out_specs=specs, check_vma=False)
```
